128 devices in a mesh: col: 16 (over y, x), row: 8 (over z, core).
Axes of the slice: x: 4, y: 4, z: 4, core: 2. Of those that a mesh axis runs over, the one named last changes fastest.
Arguments:
- matrix: float32 [24, 512, 8192], P(None, 'row', 'col'), may hold values from -0.4 to 2.4, as said below
- pivots: int32 [16, 512], replicated, may hold values from 0 to 511, as said below
- seeds: float32 [16, 512, 512], P('col'), may hold values from -1 to 2, as said below
Outputs:
- factors: float32 [24, 512, 8192], P(None, 'row', 'col')
The draws below stay inside these ranges and needn't reach their ends.
Inputs may be any that keep to these rules, and one draw needn't show every extreme that they name: Each row of pivots is an ordering of 0 .. 511. Block (r, j) of matrix is zero where r and j differ by more than 8. seeds[k] approximates the inverse of block (k, k) of matrix after the replacement of rows by pivots[k].
All inputs are finite; a program needn't handle non-finite values.
Results may differ from the reference program's by a relative error of at most 0.0001.
Values sent between devices are 32-bit elements; how exact they have to be, the bound alone decides.
No kernel may reach another device: no remote copies, remote signals or barrier semaphores. Data moves between devices by JAX's collectives and lax.ppermute only.
A program may use at most 64 MiB of HBM per device.

```python
import math
import jax
import jax.numpy as jnp
from jax import lax

B = 512
HB = 8
SWEEPS = 2
PANELS = 16
NBLK = 24
COLS = 8192


def build_all(key):
    key_perm, key_vals, key_diag, key_noise = jax.random.split(jax.random.fold_in(key, 4242), 4)
    pivots = jax.vmap(lambda one_key: jax.random.permutation(one_key, B))(jax.random.split(key_perm, PANELS)).astype(jnp.int32)
    values = jnp.clip(jax.random.normal(key_vals, (NBLK, B, COLS), jnp.float32), -4.0, 4.0)
    block_rows = jnp.arange(NBLK)[:, None, None]
    block_cols = (jnp.arange(COLS) // B)[None, None, :]
    offset = block_rows - block_cols
    spread = jnp.where(offset == 0, 0.35, 0.165) / math.sqrt(B)
    spread = jnp.where(jnp.abs(offset) <= HB, spread, 0.0)
    diag_values = jnp.exp(jax.random.uniform(key_diag, (NBLK, B), jnp.float32, 0.0, math.log(2.0)))
    on_diagonal = (jnp.arange(B)[None, :, None] == (jnp.arange(COLS) % B)[None, None, :]) & (offset == 0)
    permuted = values * spread + jnp.where(on_diagonal, diag_values[:, :, None], 0.0)
    leading = permuted[:PANELS].reshape(PANELS, B, PANELS, B)
    diag_blocks = leading[jnp.arange(PANELS), :, jnp.arange(PANELS), :]
    identity = jnp.eye(B, dtype=jnp.float32)
    approx = identity[None] / diag_values[:PANELS, None, :]
    for sweep_index in range(12):
        product = jnp.einsum('pij,pjk->pik', diag_blocks, approx, precision=lax.Precision.HIGHEST)
        approx = jnp.einsum('pij,pjk->pik', approx, 2.0 * identity[None] - product, precision=lax.Precision.HIGHEST)
    noise = jnp.clip(jax.random.normal(key_noise, (PANELS, B, B), jnp.float32), -4.0, 4.0) * (0.25 / math.sqrt(B))
    seeds = approx - jnp.einsum('pij,pjk->pik', approx, noise, precision=lax.Precision.HIGHEST)
    inverse_order = jnp.argsort(pivots, axis=1).astype(jnp.int32)
    top_rows = jnp.take_along_axis(permuted[:PANELS], inverse_order[:, :, None], axis=1)
    matrix = jnp.concatenate([top_rows, permuted[PANELS:]], axis=0)
    return (matrix, pivots, seeds)


def draw_matrix(key, part):
    return build_all(key)[0]


def draw_pivots(key, part):
    return build_all(key)[1]


def draw_seeds(key, part):
    return build_all(key)[2]


def setup_inputs(seed: int = 0) -> dict:
    key_list = jax.random.split(jax.random.key(seed), 4)
    return {
        "matrix": draw_matrix(jax.random.fold_in(key_list[3], 71), 0),
        "pivots": draw_pivots(jax.random.fold_in(key_list[3], 71), 0),
        "seeds": draw_seeds(jax.random.fold_in(key_list[3], 71), 0),
    }


def dot_high(left, right):
    return jnp.dot(left, right, precision=lax.Precision.HIGHEST, preferred_element_type=jnp.float32)


def reference(matrix, pivots, seeds):
    factors = matrix
    identity = jnp.eye(B, dtype=jnp.float32)
    column_ids = jnp.arange(COLS)
    for panel_index in range(PANELS):
        panel_cols = slice(panel_index * B, (panel_index + 1) * B)
        row_block = factors[panel_index]
        swapped = jnp.take(row_block, pivots[panel_index], axis=0)
        col_mask = (column_ids >= panel_index * B)[None, :]
        row_block = jnp.where(col_mask, swapped, row_block)
        factors = factors.at[panel_index].set(row_block)
        pivot_block = row_block[:, panel_cols]
        approx = seeds[panel_index]
        for sweep_index in range(SWEEPS):
            approx = dot_high(approx, 2.0 * identity - dot_high(pivot_block, approx))
        below_rows = factors[panel_index + 1:panel_index + HB + 1, :, panel_cols].reshape(HB * B, B)
        multipliers = dot_high(below_rows, approx)
        factors = factors.at[panel_index + 1:panel_index + HB + 1, :, panel_cols].set(multipliers.reshape(HB, B, B))
        last_panel = min(panel_index + HB, PANELS - 1)
        if last_panel >= panel_index + 1:
            trail_cols = slice((panel_index + 1) * B, (last_panel + 1) * B)
            upper_rows = row_block[:, trail_cols]
            change = dot_high(multipliers, upper_rows).reshape(HB, B, -1)
            factors = factors.at[panel_index + 1:panel_index + HB + 1, :, trail_cols].add(-change)
    return factors
```

```python
import functools

import jax
import jax.numpy as jnp
from jax import lax
from jax.experimental import pallas as pl
from jax.experimental.pallas import tpu as pltpu
from jax.sharding import PartitionSpec as P

HB = 8
PANELS = 16
B = 512
ROWS = 8
SHARE = B // ROWS
TALL = HB * SHARE

SLOT_X = {1: (0, 0), 2: (1, -1), 4: (2, -2), 5: (2, 3), 6: (2, 2)}
SLOT_Y = {2: (0, 0), 3: (1, -1), 4: (1, 2)}


def split(value):
    high = value.astype(jnp.bfloat16)
    low = (value - high.astype(jnp.float32)).astype(jnp.bfloat16)
    return high, low


def dot(left, right):
    return jnp.dot(left, right, preferred_element_type=jnp.float32)


def dot3(left, right):
    return dot(left[0], right[0]) + (dot(left[0], right[1]) + dot(left[1], right[0]))


def exact_rows(onehot, value):
    high = value.astype(jnp.bfloat16)
    rest = value - high.astype(jnp.float32)
    mid = rest.astype(jnp.bfloat16)
    low = (rest - mid.astype(jnp.float32)).astype(jnp.bfloat16)
    return dot(onehot, high) + (dot(onehot, mid) + dot(onehot, low))


def slice_offset(place, turn, swap):
    z = place // 2
    core = place % 2
    other = core if swap == 0 else 1 - core
    return (2 * ((z + 4 - turn) % 4) + other) * SHARE


def gather_copies(parts, buffer, sems, place):
    copies = []
    for index, part in enumerate(parts):
        offset = pl.multiple_of(slice_offset(place, index % 4, index // 4), SHARE)
        copies.append(pltpu.make_async_copy(part, buffer.at[pl.ds(offset, SHARE)], sems.at[index]))
    return copies


def invert_kernel(step, scal, factors_in, cur_in, y_high_ref, y_low_ref, *rest):
    parts, (factors, cur), (pivot, below, y_high, y_low, high, low, other_high, other_low, result, sems) = (
        rest[:8], rest[8:10], rest[10:])
    panel = scal[0]
    place = scal[1]

    @pl.when(panel == step)
    def _():
        copies = gather_copies(parts, pivot, sems, place)
        copies.append(pltpu.make_async_copy(y_high_ref, y_high, sems.at[8]))
        copies.append(pltpu.make_async_copy(y_low_ref, y_low, sems.at[9]))
        rows = pl.ds((step + 1) * SHARE, TALL)
        copies.append(pltpu.make_async_copy(factors_in.at[rows], below, sems.at[10]))
        for copy in copies:
            copy.start()
        for copy in copies:
            copy.wait()
        chunk = 128
        y_pair = (y_high[...], y_low[...])
        for first in range(0, B, chunk):
            block = pl.ds(first, chunk)
            product = dot3(split(pivot[block]), y_pair)
            row_ids = lax.broadcasted_iota(jnp.int32, (chunk, B), 0) + first
            col_ids = lax.broadcasted_iota(jnp.int32, (chunk, B), 1)
            error = jnp.where(row_ids == col_ids, 1.0, 0.0) - product
            high[block], low[block] = split(error)
        error_pair = (high[...], low[...])
        for first in range(0, B, chunk):
            block = pl.ds(first, chunk)
            other_high[block], other_low[block] = split(dot3((high[block], low[block]), error_pair))
            base = y_high[block].astype(jnp.float32) + y_low[block].astype(jnp.float32)
            result[block] = base + dot3((y_high[block], y_low[block]), error_pair)
        square_pair = (other_high[...], other_low[...])
        for first in range(0, B, chunk):
            block = pl.ds(first, chunk)
            base = result[block]
            high[block], low[block] = split(base + dot3(split(base), square_pair))
        inverse_pair = (high[...], low[...])
        for first in range(0, TALL, chunk):
            block = pl.ds(first, chunk)
            result[block] = dot3(split(below[block]), inverse_pair)
        to_cur = pltpu.make_async_copy(result, cur, sems.at[0])
        to_factors = pltpu.make_async_copy(result, factors.at[rows], sems.at[1])
        to_cur.start()
        to_factors.start()
        to_cur.wait()
        to_factors.wait()


def update_kernel(step, slot, scal, factors_in, cur_in, following_in, received, pivot_ref, *rest):
    parts, (factors, cur, following), (upper, multipliers, target, high, low, swapped, picks, sems) = (
        rest[:8], rest[8:11], rest[11:])
    panel = scal[0]
    place = scal[1]
    table = SLOT_X if slot == 0 else SLOT_Y
    lag = jnp.int32(0)
    takes = jnp.bool_(False)
    for distance, (amount, _) in table.items():
        if step - amount >= 0:
            here = panel == step + distance
            takes = takes | here
            lag = jnp.where(here, amount, lag)
    source = step - lag
    owns = (panel == step) if slot == 0 else jnp.bool_(False)

    @pl.when(takes | owns)
    def _():
        copies = gather_copies(parts, upper, sems, place)
        copies.append(pltpu.make_async_copy(pivot_ref.at[source], picks, sems.at[8]))
        for copy in copies:
            copy.start()

        @pl.when(takes)
        def _():
            rows = pl.ds(pl.multiple_of((source + 1) * SHARE, SHARE), TALL)
            load_m = pltpu.make_async_copy(received, multipliers, sems.at[9])
            load_t = pltpu.make_async_copy(factors_in.at[rows], target, sems.at[10])
            load_m.start()
            load_t.start()
            load_m.wait()
            load_t.wait()
        for copy in copies:
            copy.wait()

        @pl.when(takes)
        def _():
            rows = pl.ds(pl.multiple_of((source + 1) * SHARE, SHARE), TALL)
            keep = pltpu.make_async_copy(multipliers, cur, sems.at[0])
            keep.start()
            high[...], low[...] = split(upper[...])
            upper_pair = (high[...], low[...])
            for first in range(0, TALL, 128):
                block = pl.ds(first, 128)
                target[block] = target[block] - dot3(split(multipliers[block]), upper_pair)
            store_t = pltpu.make_async_copy(target, factors.at[rows], sems.at[1])
            store_n = pltpu.make_async_copy(target.at[pl.ds(0, SHARE)], following, sems.at[2])
            store_t.start()
            store_n.start()
            store_n.wait()
            store_t.wait()
            keep.wait()

        lanes = lax.broadcasted_iota(jnp.int32, (SHARE, 128), 1)
        pick = picks[...]
        onehot = jnp.concatenate(
            [jnp.where(pick == lanes + 128 * group, 1.0, 0.0) for group in range(B // 128)], axis=1
        ).astype(jnp.bfloat16)
        swapped[...] = exact_rows(onehot, upper[...])
        store = pltpu.make_async_copy(
            swapped, factors.at[pl.ds(pl.multiple_of(source * SHARE, SHARE), SHARE)], sems.at[3]
        )
        store.start()
        store.wait()


ANY = pl.BlockSpec(memory_space=pl.ANY)
SMEM = pl.BlockSpec(memory_space=pltpu.SMEM)


def f32(*shape):
    return pltpu.VMEM(shape, jnp.float32)


def b16(*shape):
    return pltpu.VMEM(shape, jnp.bfloat16)


def invert(step, scal, factors, cur, y_high, y_low, parts):
    return pl.pallas_call(
        functools.partial(invert_kernel, step),
        out_shape=[jax.ShapeDtypeStruct(a.shape, a.dtype) for a in (factors, cur)],
        in_specs=[SMEM] + [ANY] * 12,
        out_specs=[ANY] * 2,
        scratch_shapes=[f32(B, B), f32(TALL, B), b16(B, B), b16(B, B), b16(B, B), b16(B, B), b16(B, B), b16(B, B), f32(B, B),
                        pltpu.SemaphoreType.DMA((11,))],
        input_output_aliases={1: 0, 2: 1},
        compiler_params=pltpu.CompilerParams(vmem_limit_bytes=48 << 20),
    )(scal, factors, cur, y_high, y_low, *parts)


def update(step, slot, scal, factors, cur, following, received, picks, parts):
    return pl.pallas_call(
        functools.partial(update_kernel, step, slot),
        out_shape=[jax.ShapeDtypeStruct(a.shape, a.dtype) for a in (factors, cur, following)],
        in_specs=[SMEM] + [ANY] * 13,
        out_specs=[ANY] * 3,
        scratch_shapes=[f32(B, B), f32(TALL, B), f32(TALL, B), b16(B, B), b16(B, B), f32(SHARE, B),
                        pltpu.VMEM((SHARE, 128), jnp.int32), pltpu.SemaphoreType.DMA((11,))],
        input_output_aliases={1: 0, 2: 1, 3: 2},
        compiler_params=pltpu.CompilerParams(vmem_limit_bytes=48 << 20),
    )(scal, factors, cur, following, received, picks, *parts)


def gather(share, panels):
    def move(array, target):
        pairs = [(c * ROWS + r, c * ROWS + target(r)) for c in panels for r in range(ROWS)]
        return lax.ppermute(array, ("col", "row"), pairs)

    turned = [share] + [move(share, lambda r, t=turn: (r + 2 * t) % ROWS) for turn in (1, 2, 3)]
    return turned + [move(part, lambda r: r ^ 1) for part in turned]


def send(cur, step, table):
    pairs = []
    for distance, (lag, sender) in table.items():
        if step - lag >= 0 and step + distance < PANELS:
            for r in range(ROWS):
                pairs.append(((step + sender) * ROWS + r, (step + distance) * ROWS + r))
    return lax.ppermute(cur, ("col", "row"), pairs)


def in_slot(step, table):
    return [step + d for d, (lag, _) in table.items() if step - lag >= 0 and step + d < PANELS]


def local(matrix, pivots, seeds):
    panel = lax.axis_index("col")
    place = lax.axis_index("row")
    scal = jnp.stack([panel, place]).astype(jnp.int32)
    factors = matrix.reshape(-1, B)
    own_pivots = lax.dynamic_index_in_dim(pivots, panel, 0, keepdims=False)
    onehot = (own_pivots[:, None] == jnp.arange(B, dtype=jnp.int32)[None, :]).astype(jnp.float32)
    start = jnp.dot(seeds[0], onehot, precision=lax.Precision.HIGHEST, preferred_element_type=jnp.float32)
    y_high, y_low = split(start)
    picks = jnp.broadcast_to(
        lax.dynamic_slice_in_dim(pivots, place * SHARE, SHARE, 1)[:, :, None], (PANELS, SHARE, 128)
    )
    first = jnp.maximum(panel - HB, 0)
    following = lax.dynamic_slice_in_dim(factors, first * SHARE, SHARE, 0)
    cur = jnp.zeros((TALL, B), jnp.float32)
    for step in range(PANELS):
        parts = gather(following, [step] + in_slot(step, SLOT_X))
        factors, cur = invert(step, scal, factors, cur, y_high, y_low, parts)
        panels = in_slot(step, SLOT_X)
        received = send(cur, step, SLOT_X) if panels else cur
        factors, cur, following = update(step, 0, scal, factors, cur, following, received, picks, parts)
        panels = in_slot(step, SLOT_Y)
        if panels:
            parts = gather(following, panels)
            received = send(cur, step, SLOT_Y)
            factors, cur, following = update(step, 1, scal, factors, cur, following, received, picks, parts)
    at = (panel + 1) * SHARE
    own = lax.dynamic_slice_in_dim(factors, at, TALL, 0)
    own = lax.dot_general(
        own, onehot, (((1,), (1,)), ((), ())), precision=lax.Precision.HIGHEST, preferred_element_type=jnp.float32
    )
    factors = lax.dynamic_update_slice_in_dim(factors, own, at, 0)
    return factors.reshape(matrix.shape)


def solution(mesh):
    return jax.shard_map(
        local,
        mesh=mesh,
        in_specs=(P(None, "row", "col"), P(), P("col", None, None)),
        out_specs=P(None, "row", "col"),
        check_vma=False,
    )
```

```python
import functools

import jax
import jax.numpy as jnp
from jax import lax
from jax.experimental import pallas as pl
from jax.experimental.pallas import tpu as pltpu
from jax.sharding import PartitionSpec as P

HB = 8
PANELS = 16
B = 512
ROWS = 8
SHARE = B // ROWS
TALL = HB * SHARE
TILE = 9

SLOT_X = {1: (0, 0), 2: (1, -1), 4: (2, -2), 5: (2, 3), 6: (2, 2)}
SLOT_Y = {2: (0, 0), 3: (1, -1), 4: (1, 2)}


def split(value):
    high = value.astype(jnp.bfloat16)
    low = (value - high.astype(jnp.float32)).astype(jnp.bfloat16)
    return high, low


def dot(left, right):
    return jnp.dot(left, right, preferred_element_type=jnp.float32)


def dot3(left, right):
    return dot(left[0], right[0]) + (dot(left[0], right[1]) + dot(left[1], right[0]))


def exact_rows(onehot, value):
    high = value.astype(jnp.bfloat16)
    rest = value - high.astype(jnp.float32)
    mid = rest.astype(jnp.bfloat16)
    low = (rest - mid.astype(jnp.float32)).astype(jnp.bfloat16)
    return dot(onehot, high) + (dot(onehot, mid) + dot(onehot, low))


def invert_kernel(step, scal, factors_in, cur_in, upper_in, y_high_ref, y_low_ref, factors, cur,
                  pivot, below, y_high, y_low, high, low, other_high, other_low, result, sems):
    rows = pl.ds((step + 1) * SHARE, TALL)
    load = [
        pltpu.make_async_copy(upper_in, pivot, sems.at[0]),
        pltpu.make_async_copy(y_high_ref, y_high, sems.at[1]),
        pltpu.make_async_copy(y_low_ref, y_low, sems.at[2]),
        pltpu.make_async_copy(factors_in.at[rows], below, sems.at[3]),
    ]
    for copy in load:
        copy.start()
    for copy in load[:3]:
        copy.wait()
    chunk = 256

    def errors(index, _):
        first = pl.multiple_of(index * chunk, chunk)
        block = pl.ds(first, chunk)
        product = dot3(split(pivot[block]), (y_high[...], y_low[...]))
        row_ids = lax.broadcasted_iota(jnp.int32, (chunk, B), 0) + first
        col_ids = lax.broadcasted_iota(jnp.int32, (chunk, B), 1)
        high[block], low[block] = split(jnp.where(row_ids == col_ids, 1.0, 0.0) - product)
        return 0

    def squares(index, _):
        block = pl.ds(pl.multiple_of(index * chunk, chunk), chunk)
        other_high[block], other_low[block] = split(dot3((high[block], low[block]), (high[...], low[...])))
        base = y_high[block].astype(jnp.float32) + y_low[block].astype(jnp.float32)
        result[block] = base + dot3((y_high[block], y_low[block]), (high[...], low[...]))
        return 0

    def inverses(index, _):
        block = pl.ds(pl.multiple_of(index * chunk, chunk), chunk)
        base = result[block]
        high[block], low[block] = split(base + dot3(split(base), (other_high[...], other_low[...])))
        return 0

    def multipliers(index, _):
        block = pl.ds(pl.multiple_of(index * chunk, chunk), chunk)
        result[block] = dot3(split(below[block]), (high[...], low[...]))
        return 0

    lax.fori_loop(0, B // chunk, errors, 0)
    lax.fori_loop(0, B // chunk, squares, 0)
    lax.fori_loop(0, B // chunk, inverses, 0)
    load[3].wait()
    lax.fori_loop(0, TALL // chunk, multipliers, 0)
    store = [pltpu.make_async_copy(result, cur, sems.at[0]), pltpu.make_async_copy(result, factors.at[rows], sems.at[1])]
    for copy in store:
        copy.start()
    for copy in store:
        copy.wait()


def lag_of(step, table, panel):
    lag = jnp.int32(0)
    for distance, (amount, _) in table.items():
        if amount:
            lag = jnp.where(panel == step + distance, amount, lag)
    return lag


def update_kernel(step, slot, scal, factors_in, cur_in, upper_in, received, factors, cur, following,
                  upper, multipliers, target, high, low, sems):
    panel = scal[0]
    table = SLOT_X if slot == 0 else SLOT_Y
    source = step - lag_of(step, table, panel)
    rows = pl.ds(pl.multiple_of((source + 1) * SHARE, SHARE), TALL)
    load = [
        pltpu.make_async_copy(upper_in, upper, sems.at[0]),
        pltpu.make_async_copy(received, multipliers, sems.at[1]),
        pltpu.make_async_copy(factors_in.at[rows], target, sems.at[2]),
    ]
    for copy in load:
        copy.start()
    load[0].wait()
    high[...], low[...] = split(upper[...])
    load[1].wait()
    keep = pltpu.make_async_copy(multipliers, cur, sems.at[3])
    keep.start()
    load[2].wait()
    chunk = 256

    def subtract(index, _):
        block = pl.ds(pl.multiple_of(index * chunk, chunk), chunk)
        target[block] = target[block] - dot3(split(multipliers[block]), (high[...], low[...]))
        return 0

    lax.fori_loop(0, TALL // chunk, subtract, 0)
    store = [
        pltpu.make_async_copy(target.at[pl.ds(0, SHARE)], following, sems.at[0]),
        pltpu.make_async_copy(target, factors.at[rows], sems.at[1]),
    ]
    for copy in store:
        copy.start()
    for copy in store:
        copy.wait()
    keep.wait()


def place_kernel(scal, factors_in, upper_in, pivot_ref, *rest):
    parts, (factors, upper_out), (upper, swapped, picks, sems) = rest[:8], rest[8:10], rest[10:]
    del upper_in
    place = scal[1]
    source = scal[2]
    z = place // 2
    core = place % 2
    load = []
    for index, part in enumerate(parts):
        other = core if index < 4 else 1 - core
        offset = (2 * ((z + 4 - index % 4) % 4) + other) * SHARE
        load.append(pltpu.make_async_copy(part, upper.at[pl.ds(pl.multiple_of(offset, SHARE), SHARE)], sems.at[index]))
    load.append(pltpu.make_async_copy(pivot_ref.at[source], picks, sems.at[8]))
    for copy in load:
        copy.start()
    for copy in load:
        copy.wait()
    keep = pltpu.make_async_copy(upper, upper_out, sems.at[0])
    keep.start()
    lanes = lax.broadcasted_iota(jnp.int32, (SHARE, 128), 1)
    pick = picks[...]
    onehot = jnp.concatenate(
        [jnp.where(pick == lanes + 128 * group, 1.0, 0.0) for group in range(B // 128)], axis=1
    ).astype(jnp.bfloat16)
    swapped[...] = exact_rows(onehot, upper[...])
    at = pl.ds(pl.multiple_of(source * SHARE, SHARE), SHARE)
    store = pltpu.make_async_copy(swapped, factors.at[at], sems.at[1])
    store.start()
    store.wait()
    keep.wait()


ANY = pl.BlockSpec(memory_space=pl.ANY)
SMEM = pl.BlockSpec(memory_space=pltpu.SMEM)


def f32(*shape):
    return pltpu.VMEM(shape, jnp.float32)


def b16(*shape):
    return pltpu.VMEM(shape, jnp.bfloat16)


def like(*arrays):
    return [jax.ShapeDtypeStruct(a.shape, a.dtype) for a in arrays]


def invert(step, scal, factors, cur, upper, y_high, y_low):
    return pl.pallas_call(
        functools.partial(invert_kernel, step),
        out_shape=like(factors, cur),
        in_specs=[SMEM] + [ANY] * 5,
        out_specs=[ANY] * 2,
        scratch_shapes=[f32(B, B), f32(TALL, B)] + [b16(B, B)] * 6 + [f32(B, B), pltpu.SemaphoreType.DMA((4,))],
        input_output_aliases={1: 0, 2: 1},
        compiler_params=pltpu.CompilerParams(vmem_limit_bytes=48 << 20),
    )(scal, factors, cur, upper, y_high, y_low)


def update(step, slot, scal, factors, cur, upper, received):
    return pl.pallas_call(
        functools.partial(update_kernel, step, slot),
        out_shape=like(factors, cur) + [jax.ShapeDtypeStruct((SHARE, B), jnp.float32)],
        in_specs=[SMEM] + [ANY] * 4,
        out_specs=[ANY] * 3,
        scratch_shapes=[f32(B, B), f32(TALL, B), f32(TALL, B), b16(B, B), b16(B, B), pltpu.SemaphoreType.DMA((4,))],
        input_output_aliases={1: 0, 2: 1},
        compiler_params=pltpu.CompilerParams(vmem_limit_bytes=48 << 20),
    )(scal, factors, cur, upper, received)


def put_in_place(scal, factors, upper, picks, parts):
    return pl.pallas_call(
        place_kernel,
        out_shape=like(factors, upper),
        in_specs=[SMEM] + [ANY] * 11,
        out_specs=[ANY] * 2,
        scratch_shapes=[f32(B, B), f32(SHARE, B), pltpu.VMEM((SHARE, 128), jnp.int32), pltpu.SemaphoreType.DMA((9,))],
        input_output_aliases={1: 0, 2: 1},
        compiler_params=pltpu.CompilerParams(vmem_limit_bytes=48 << 20),
    )(scal, factors, upper, picks, *parts)


def gather(share):
    turned = [share] + [
        lax.ppermute(share, "row", [(r, (r + 2 * turn) % ROWS) for r in range(ROWS)]) for turn in (1, 2, 3)
    ]
    return turned + [lax.ppermute(part, "row", [(r, r ^ 1) for r in range(ROWS)]) for part in turned]


def send(cur, step, table):
    first = step % TILE - TILE
    pairs = []
    for at in range(first, PANELS + TILE, TILE):
        for distance, (_, sender) in table.items():
            if at + sender in range(PANELS) and at + distance in range(PANELS):
                pairs += [((at + sender) * ROWS + r, (at + distance) * ROWS + r) for r in range(ROWS)]
    return lax.ppermute(cur, ("col", "row"), pairs)


def members(step, table):
    takers = [step + d for d, (lag, _) in table.items() if step - lag >= 0 and step + d < PANELS]
    inside = set(takers)
    grown = True
    while grown:
        grown = False
        for distance, (_, sender) in table.items():
            pair = {step + sender, step + distance}
            if pair <= set(range(PANELS)) and pair & inside and not pair <= inside:
                inside |= pair
                grown = True
    return takers, sorted(inside)


def among(panel, panels):
    hit = panel == panels[0]
    for other in panels[1:]:
        hit = hit | (panel == other)
    return hit


def local(matrix, pivots, seeds):
    panel = lax.axis_index("col").astype(jnp.int32)
    place = lax.axis_index("row").astype(jnp.int32)
    factors = matrix.reshape(-1, B)
    own_pivots = lax.dynamic_index_in_dim(pivots, panel, 0, keepdims=False)
    onehot = (own_pivots[:, None] == jnp.arange(B, dtype=jnp.int32)[None, :]).astype(jnp.float32)
    start = jnp.dot(seeds[0], onehot, precision=lax.Precision.HIGHEST, preferred_element_type=jnp.float32)
    y_high, y_low = split(start)
    picks = jnp.broadcast_to(
        lax.dynamic_slice_in_dim(pivots, place * SHARE, SHARE, 1)[:, :, None], (PANELS, SHARE, 128)
    )
    first = jnp.maximum(panel - HB, 0)
    following = lax.dynamic_slice_in_dim(factors, first * SHARE, SHARE, 0)
    cur = jnp.zeros((TALL, B), jnp.float32)
    upper = jnp.zeros((B, B), jnp.float32)
    factors, upper = put_in_place(jnp.stack([panel, place, first]), factors, upper, picks, gather(following))

    def slot(step, index, factors, cur, upper):
        table = (SLOT_X, SLOT_Y)[index]
        takers, inside = members(step, table)
        if not takers:
            return factors, cur, upper

        def exchange(factors, cur, upper):
            received = send(cur, step, table)

            def take(factors, cur, upper, received):
                new_factors, new_cur, following = update(
                    step, index, jnp.stack([panel, place]), factors, cur, upper, received
                )
                at = jnp.stack([panel, place, step + 1 - lag_of(step, table, panel)])
                new_factors, new_upper = put_in_place(at, new_factors, upper, picks, gather(following))
                return new_factors, new_cur, new_upper

            return lax.cond(
                among(panel, takers), take, lambda factors, cur, upper, received: (factors, cur, upper),
                factors, cur, upper, received,
            )

        return lax.cond(among(panel, inside), exchange, lambda *state: state, factors, cur, upper)

    for step in range(PANELS):
        factors, cur = lax.cond(
            panel == step,
            lambda factors, cur, upper: tuple(invert(step, jnp.stack([panel, place]), factors, cur, upper, y_high, y_low)),
            lambda factors, cur, upper: (factors, cur),
            factors, cur, upper,
        )
        factors, cur, upper = slot(step, 0, factors, cur, upper)
        factors, cur, upper = slot(step, 1, factors, cur, upper)
    at = (panel + 1) * SHARE
    own = lax.dynamic_slice_in_dim(factors, at, TALL, 0)
    own = lax.dot_general(
        own, onehot, (((1,), (1,)), ((), ())), precision=lax.Precision.HIGHEST, preferred_element_type=jnp.float32
    )
    factors = lax.dynamic_update_slice_in_dim(factors, own, at, 0)
    return factors.reshape(matrix.shape)


def solution(mesh):
    return jax.shard_map(
        local,
        mesh=mesh,
        in_specs=(P(None, "row", "col"), P(), P("col", None, None)),
        out_specs=P(None, "row", "col"),
        check_vma=False,
    )
```

```python
import functools

import jax
import jax.numpy as jnp
from jax import lax
from jax.experimental import pallas as pl
from jax.experimental.pallas import tpu as pltpu
from jax.sharding import PartitionSpec as P

HB = 8
PANELS = 16
B = 512
ROWS = 8
SHARE = B // ROWS
TALL = HB * SHARE
TILE = 9

NEAR = {1: (0, 0), 2: (1, -1), 3: (2, -2), 4: (2, 2)}
FAR = {2: (0, 0), 3: (1, -1), 5: (2, -2), 6: (2, 2)}


def split(value):
    high = value.astype(jnp.bfloat16)
    low = (value - high.astype(jnp.float32)).astype(jnp.bfloat16)
    return high, low


def dot(left, right):
    return jnp.dot(left, right, preferred_element_type=jnp.float32)


def dot3(left, right):
    return dot(left[0], right[0]) + (dot(left[0], right[1]) + dot(left[1], right[0]))


def exact_rows(onehot, value):
    high = value.astype(jnp.bfloat16)
    rest = value - high.astype(jnp.float32)
    mid = rest.astype(jnp.bfloat16)
    low = (rest - mid.astype(jnp.float32)).astype(jnp.bfloat16)
    return dot(onehot, high) + (dot(onehot, mid) + dot(onehot, low))


def split_into(value, high, low):
    def rows(index, _):
        block = pl.ds(pl.multiple_of(index * SHARE, SHARE), SHARE)
        high[block], low[block] = split(value[block])
        return 0

    lax.fori_loop(0, B // SHARE, rows, 0)


def halves_kernel(value_ref, high_ref, low_ref, value, high, low, sems):
    load = pltpu.make_async_copy(value_ref, value, sems.at[0])
    load.start()
    load.wait()
    split_into(value, high, low)
    store = [pltpu.make_async_copy(high, high_ref, sems.at[0]), pltpu.make_async_copy(low, low_ref, sems.at[1])]
    for copy in store:
        copy.start()
    for copy in store:
        copy.wait()


def inverse_kernel(pivot_ref, y_high_ref, y_low_ref, high_ref, low_ref,
                   pivot, y_high, y_low, high, low, other_high, other_low, result, sems):
    load = [
        pltpu.make_async_copy(pivot_ref, pivot, sems.at[0]),
        pltpu.make_async_copy(y_high_ref, y_high, sems.at[1]),
        pltpu.make_async_copy(y_low_ref, y_low, sems.at[2]),
    ]
    for copy in load:
        copy.start()
    for copy in load:
        copy.wait()
    chunk = 128

    def errors(index, _):
        first = pl.multiple_of(index * chunk, chunk)
        block = pl.ds(first, chunk)
        product = dot3(split(pivot[block]), (y_high[...], y_low[...]))
        row_ids = lax.broadcasted_iota(jnp.int32, (chunk, B), 0) + first
        col_ids = lax.broadcasted_iota(jnp.int32, (chunk, B), 1)
        high[block], low[block] = split(jnp.where(row_ids == col_ids, 1.0, 0.0) - product)
        return 0

    def squares(index, _):
        block = pl.ds(pl.multiple_of(index * chunk, chunk), chunk)
        other_high[block], other_low[block] = split(dot3((high[block], low[block]), (high[...], low[...])))
        base = y_high[block].astype(jnp.float32) + y_low[block].astype(jnp.float32)
        result[block] = base + dot3((y_high[block], y_low[block]), (high[...], low[...]))
        return 0

    def inverses(index, _):
        block = pl.ds(pl.multiple_of(index * chunk, chunk), chunk)
        base = result[block]
        high[block], low[block] = split(base + dot3(split(base), (other_high[...], other_low[...])))
        return 0

    lax.fori_loop(0, B // chunk, errors, 0)
    lax.fori_loop(0, B // chunk, squares, 0)
    lax.fori_loop(0, B // chunk, inverses, 0)
    store = [pltpu.make_async_copy(high, high_ref, sems.at[0]), pltpu.make_async_copy(low, low_ref, sems.at[1])]
    for copy in store:
        copy.start()
    for copy in store:
        copy.wait()


def multiply_kernel(owner, factors_in, cur_in, upper_in, received, high_ref, low_ref, factors, cur, front,
                    upper, multipliers, below, high, low, upper_high, upper_low, sems):
    rows = pl.ds((owner + 1) * SHARE, TALL)
    load = [
        pltpu.make_async_copy(factors_in.at[rows], below, sems.at[0]),
        pltpu.make_async_copy(high_ref, high, sems.at[1]),
        pltpu.make_async_copy(low_ref, low, sems.at[2]),
    ]
    if owner:
        load += [
            pltpu.make_async_copy(upper_in, upper, sems.at[3]),
            pltpu.make_async_copy(received, multipliers, sems.at[4]),
        ]
    for copy in load:
        copy.start()
    if owner:
        load[3].wait()
        split_into(upper, upper_high, upper_low)
    for copy in load[:3] + load[4:]:
        copy.wait()
    if owner:
        chunk = (TALL - SHARE) // 2

        def subtract(index, _):
            first = pl.multiple_of(index * chunk, 32)
            block = pl.ds(first, chunk)
            shifted = pl.ds(pl.multiple_of(first + SHARE, 32), chunk)
            below[block] = below[block] - dot3(split(multipliers[shifted]), (upper_high[...], upper_low[...]))
            return 0

        lax.fori_loop(0, 2, subtract, 0)
    part = 128

    def multiply(index, _):
        block = pl.ds(pl.multiple_of(index * part, part), part)
        below[block] = dot3(split(below[block]), (high[...], low[...]))
        return 0

    lax.fori_loop(0, TALL // part, multiply, 0)
    store = [
        pltpu.make_async_copy(below.at[pl.ds(0, SHARE)], front, sems.at[0]),
        pltpu.make_async_copy(below, cur, sems.at[1]),
        pltpu.make_async_copy(below, factors.at[rows], sems.at[2]),
    ]
    for copy in store:
        copy.start()
    for copy in store:
        copy.wait()


def front_kernel(step, factors_in, upper_in, received, following, upper, multipliers, target, high, low, sems):
    rows = pl.ds((step + 1) * SHARE, SHARE)
    load = [
        pltpu.make_async_copy(upper_in, upper, sems.at[0]),
        pltpu.make_async_copy(received, multipliers, sems.at[1]),
        pltpu.make_async_copy(factors_in.at[rows], target, sems.at[2]),
    ]
    for copy in load:
        copy.start()
    for copy in load:
        copy.wait()
    left = split(multipliers[...])
    split_into(upper, high, low)
    target[...] = target[...] - dot3(left, (high[...], low[...]))
    store = pltpu.make_async_copy(target, following, sems.at[0])
    store.start()
    store.wait()


def lag_of(step, table, panel):
    lag = jnp.int32(0)
    for distance, (amount, _) in table.items():
        if amount:
            lag = jnp.where(panel == step + distance, amount, lag)
    return lag


def update_kernel(step, far, scal, factors_in, cur_in, upper_in, received, factors, cur, following,
                  upper, multipliers, target, high, low, sems):
    panel = scal[0]
    source = step - lag_of(step, FAR if far else NEAR, panel)
    rows = pl.ds(pl.multiple_of((source + 1) * SHARE, SHARE), TALL)
    load = [
        pltpu.make_async_copy(upper_in, upper, sems.at[0]),
        pltpu.make_async_copy(received, multipliers, sems.at[1]),
        pltpu.make_async_copy(factors_in.at[rows], target, sems.at[2]),
    ]
    for copy in load:
        copy.start()
    load[0].wait()
    split_into(upper, high, low)
    load[1].wait()
    if far:
        keep = pltpu.make_async_copy(multipliers, cur, sems.at[3])
        keep.start()
    load[2].wait()
    chunk = 128

    def subtract(index, _):
        block = pl.ds(pl.multiple_of(index * chunk, chunk), chunk)
        target[block] = target[block] - dot3(split(multipliers[block]), (high[...], low[...]))
        return 0

    lax.fori_loop(0, TALL // chunk, subtract, 0)
    store = [
        pltpu.make_async_copy(target.at[pl.ds(0, SHARE)], following, sems.at[0]),
        pltpu.make_async_copy(target, factors.at[rows], sems.at[1]),
    ]
    for copy in store:
        copy.start()
    for copy in store:
        copy.wait()
    if far:
        keep.wait()


def place_kernel(scal, factors_in, pivot_ref, *rest):
    parts, (factors, upper_out), (upper, swapped, picks, sems) = rest[:8], rest[8:10], rest[10:]
    place = scal[1]
    source = scal[2]
    z = place // 2
    core = place % 2
    load = []
    for index, part in enumerate(parts):
        other = core if index < 4 else 1 - core
        offset = (2 * ((z + 4 - index % 4) % 4) + other) * SHARE
        load.append(pltpu.make_async_copy(part, upper.at[pl.ds(pl.multiple_of(offset, SHARE), SHARE)], sems.at[index]))
    load.append(pltpu.make_async_copy(pivot_ref.at[source], picks, sems.at[8]))
    for copy in load:
        copy.start()
    for copy in load:
        copy.wait()
    keep = pltpu.make_async_copy(upper, upper_out, sems.at[0])
    keep.start()
    lanes = lax.broadcasted_iota(jnp.int32, (SHARE, 128), 1)
    swapped[...] = jnp.zeros_like(swapped)

    def pick_rows(group, _):
        onehot = jnp.where(picks[...] == lanes + 128 * group, 1.0, 0.0).astype(jnp.bfloat16)
        block = pl.ds(pl.multiple_of(group * 128, 128), 128)
        swapped[...] = swapped[...] + exact_rows(onehot, upper[block])
        return 0

    lax.fori_loop(0, B // 128, pick_rows, 0)
    at = pl.ds(pl.multiple_of(source * SHARE, SHARE), SHARE)
    store = pltpu.make_async_copy(swapped, factors.at[at], sems.at[1])
    store.start()
    store.wait()
    keep.wait()


ANY = pl.BlockSpec(memory_space=pl.ANY)
SMEM = pl.BlockSpec(memory_space=pltpu.SMEM)


def f32(*shape):
    return pltpu.VMEM(shape, jnp.float32)


def b16(*shape):
    return pltpu.VMEM(shape, jnp.bfloat16)


def like(*arrays):
    return [jax.ShapeDtypeStruct(a.shape, a.dtype) for a in arrays]


def call(kernel, out_shape, scratch, aliases, *operands, scal=None):
    first = [] if scal is None else [scal]
    return pl.pallas_call(
        kernel,
        out_shape=out_shape,
        in_specs=[SMEM] * len(first) + [ANY] * len(operands),
        out_specs=[ANY] * len(out_shape),
        scratch_shapes=scratch,
        input_output_aliases=aliases,
        compiler_params=pltpu.CompilerParams(vmem_limit_bytes=48 << 20),
    )(*first, *operands)


def inverse(pivot, y_high, y_low):
    scratch = [f32(B, B)] + [b16(B, B)] * 6 + [f32(B, B), pltpu.SemaphoreType.DMA((3,))]
    return call(inverse_kernel, like(y_high, y_low), scratch, {}, pivot, y_high, y_low)


def multiply(owner, factors, cur, front, upper, received, high, low):
    scratch = [f32(B, B), f32(TALL, B), f32(TALL, B)] + [b16(B, B)] * 4 + [pltpu.SemaphoreType.DMA((5,))]
    return call(functools.partial(multiply_kernel, owner), like(factors, cur, front), scratch, {0: 0, 1: 1},
                factors, cur, upper, received, high, low)


def advance(step, factors, following, upper, received):
    scratch = [f32(B, B), f32(SHARE, B), f32(SHARE, B), b16(B, B), b16(B, B), pltpu.SemaphoreType.DMA((3,))]
    return call(functools.partial(front_kernel, step), like(following), scratch, {}, factors, upper, received)[0]


def update(step, far, scal, factors, cur, following, upper, received):
    scratch = [f32(B, B), f32(TALL, B), f32(TALL, B), b16(B, B), b16(B, B), pltpu.SemaphoreType.DMA((4,))]
    outs = like(factors, cur, following) if far else like(factors, following)
    kernel = functools.partial(update_kernel if far else near_kernel, step, far)
    return call(kernel, outs, scratch, {1: 0, 2: 1} if far else {1: 0}, factors, cur, upper, received, scal=scal) if far else call(
        kernel, outs, scratch, {1: 0}, factors, upper, received, scal=scal)


def near_kernel(step, far, scal, factors_in, upper_in, received, factors, following, *scratch):
    update_kernel(step, far, scal, factors_in, None, upper_in, received, factors, None, following, *scratch)


def put_in_place(scal, factors, upper, picks, parts):
    scratch = [f32(B, B), f32(SHARE, B), pltpu.VMEM((SHARE, 128), jnp.int32), pltpu.SemaphoreType.DMA((9,))]
    return call(place_kernel, like(factors, upper), scratch, {1: 0}, factors, picks, *parts, scal=scal)


def gather(share):
    turned = [share] + [
        lax.ppermute(share, "row", [(r, (r + 2 * turn) % ROWS) for r in range(ROWS)]) for turn in (1, 2, 3)
    ]
    return turned + [lax.ppermute(part, "row", [(r, r ^ 1) for r in range(ROWS)]) for part in turned]


def send(cur, step, table):
    first = step % TILE - TILE
    pairs = []
    for at in range(first, PANELS + TILE, TILE):
        for distance, (_, sender) in table.items():
            if at + sender in range(PANELS) and at + distance in range(PANELS):
                pairs += [((at + sender) * ROWS + r, (at + distance) * ROWS + r) for r in range(ROWS)]
    return lax.ppermute(cur, ("col", "row"), pairs)


def members(step, tables):
    takers = sorted({
        step + d for table in tables for d, (lag, _) in table.items() if step - lag >= 0 and step + d < PANELS
    })
    inside = set(takers)
    grown = True
    while grown:
        grown = False
        for table in tables:
            for distance, (_, sender) in table.items():
                pair = {step + sender, step + distance}
                if pair <= set(range(PANELS)) and pair & inside and not pair <= inside:
                    inside |= pair
                    grown = True
    return takers, sorted(inside)


def shifted(odd):
    return [(c * ROWS + r, (c + 1) * ROWS + r) for c in range(odd, PANELS - 1, 2) for r in range(ROWS)]


def among(panel, panels):
    hit = panel == panels[0]
    for other in panels[1:]:
        hit = hit | (panel == other)
    return hit


def local(matrix, pivots, seeds):
    panel = lax.axis_index("col").astype(jnp.int32)
    place = lax.axis_index("row").astype(jnp.int32)
    factors = matrix.reshape(-1, B)
    own_pivots = lax.dynamic_index_in_dim(pivots, panel, 0, keepdims=False)
    onehot = (own_pivots[:, None] == jnp.arange(B, dtype=jnp.int32)[None, :]).astype(jnp.float32)
    start = jnp.dot(seeds[0], onehot, precision=lax.Precision.HIGHEST, preferred_element_type=jnp.float32)
    half = jax.ShapeDtypeStruct((B, B), jnp.bfloat16)
    y_high, y_low = call(halves_kernel, [half, half], [f32(B, B), b16(B, B), b16(B, B), pltpu.SemaphoreType.DMA((2,))], {}, start)
    picks = jnp.broadcast_to(
        lax.dynamic_slice_in_dim(pivots, place * SHARE, SHARE, 1)[:, :, None], (PANELS, SHARE, 128)
    )
    first = jnp.maximum(panel - HB, 0)
    following = lax.dynamic_slice_in_dim(factors, first * SHARE, SHARE, 0)
    cur = jnp.zeros((TALL, B), jnp.float32)
    front = jnp.zeros((SHARE, B), jnp.float32)
    where = jnp.stack([panel, place])

    def when(panels, run, *state):
        if not panels:
            return state
        return lax.cond(among(panel, panels), lambda *state: tuple(run(*state)), lambda *state: state, *state)

    def collect(source, factors, upper, following):
        return put_in_place(jnp.stack([panel, place, source]), factors, upper, picks, gather(following))

    upper = jnp.zeros((B, B), jnp.float32)

    def begin(factors, cur, front, upper):
        factors, upper = collect(panel, factors, upper, following)
        factors, cur, front = multiply(0, factors, cur, front, upper, cur, *inverse(upper, y_high, y_low))
        return factors, cur, front, upper

    factors, cur, front, upper = when([0], begin, factors, cur, front, upper)

    for step in range(PANELS - 1):
        coming = step + 1

        def prepare(factors, upper):
            return collect(step, factors, upper, following)

        factors, upper = when([coming], prepare, factors, upper)

        def lead(following):
            arrived = lax.ppermute(front, ("col", "row"), shifted(step % 2))
            return (advance(step, factors, following, upper, arrived),)

        (following,) = when([step, coming], lead, following)
        near, _ = members(step, [NEAR])
        far, _ = members(step, [FAR])
        _, inside = members(step, [NEAR, FAR])

        def exchange(factors, cur, front, upper, following):
            p = send(cur, step, NEAR)
            q = send(cur, step, FAR) if far else None
            source = jnp.where(
                panel == coming, coming, jnp.maximum(step - lag_of(step, FAR | NEAR, panel), 0)
            )

            def bring(factors, fresh):
                return collect(source, factors, upper, following)

            factors, fresh = when(sorted(set(near) | set(far)), bring, factors, upper)
            high, low = inverse(fresh, y_high, y_low)

            def near_update(factors, following):
                return update(step, False, where, factors, cur, following, fresh, p)

            factors, following = when([c for c in near if c != coming], near_update, factors, following)

            def again(factors, fresh):
                return collect(step + 1 - lag_of(step, NEAR, panel), factors, fresh, following)

            factors, fresh = when(sorted(set(near) & set(far)), again, factors, fresh)

            def far_update(factors, new_cur, following):
                return update(step, True, where, factors, new_cur, following, fresh, q)

            factors, new_cur, following = when(far, far_update, factors, cur, following)

            def own(factors, cur, front):
                return multiply(coming, factors, cur, front, upper, p, high, low)

            factors, new_cur, front = when([coming], own, factors, new_cur, front)
            return factors, new_cur, front, fresh, following

        factors, cur, front, upper, following = when(inside, exchange, factors, cur, front, upper, following)
    at = (panel + 1) * SHARE
    own = lax.dynamic_slice_in_dim(factors, at, TALL, 0)
    own = lax.dot_general(
        own, onehot, (((1,), (1,)), ((), ())), precision=lax.Precision.HIGHEST, preferred_element_type=jnp.float32
    )
    factors = lax.dynamic_update_slice_in_dim(factors, own, at, 0)
    return factors.reshape(matrix.shape)


def solution(mesh):
    return jax.shard_map(
        local,
        mesh=mesh,
        in_specs=(P(None, "row", "col"), P(), P("col", None, None)),
        out_specs=P(None, "row", "col"),
        check_vma=False,
    )
```

```python
import functools

import jax
import jax.numpy as jnp
from jax import lax
from jax.experimental import pallas as pl
from jax.experimental.pallas import tpu as pltpu
from jax.sharding import PartitionSpec as P

HB = 8
PANELS = 16
B = 512
ROWS = 8
SHARE = B // ROWS
TALL = HB * SHARE
TILE = 9

NEAR = {1: (0, 0), 2: (1, -1), 3: (2, -2), 4: (2, 2)}
FAR = {2: (0, 0), 3: (1, -1), 5: (2, -2), 6: (2, 2)}


def split(value):
    high = value.astype(jnp.bfloat16)
    low = (value - high.astype(jnp.float32)).astype(jnp.bfloat16)
    return high, low


def dot(left, right):
    return jnp.dot(left, right, preferred_element_type=jnp.float32)


def dot3(left, right):
    return dot(left[0], right[0]) + (dot(left[0], right[1]) + dot(left[1], right[0]))


def exact_rows(onehot, value):
    high = value.astype(jnp.bfloat16)
    rest = value - high.astype(jnp.float32)
    mid = rest.astype(jnp.bfloat16)
    low = (rest - mid.astype(jnp.float32)).astype(jnp.bfloat16)
    return dot(onehot, high) + (dot(onehot, mid) + dot(onehot, low))


def split_into(value, high, low):
    def rows(index, _):
        block = pl.ds(pl.multiple_of(index * SHARE, SHARE), SHARE)
        high[block], low[block] = split(value[block])
        return 0

    lax.fori_loop(0, B // SHARE, rows, 0)


def halves_kernel(value_ref, high_ref, low_ref, value, high, low, sems):
    load = pltpu.make_async_copy(value_ref, value, sems.at[0])
    load.start()
    load.wait()
    split_into(value, high, low)
    store = [pltpu.make_async_copy(high, high_ref, sems.at[0]), pltpu.make_async_copy(low, low_ref, sems.at[1])]
    for copy in store:
        copy.start()
    for copy in store:
        copy.wait()


def inverse_kernel(pivot_ref, y_high_ref, y_low_ref, high_ref, low_ref,
                   pivot, y_high, y_low, high, low, other_high, other_low, result, sems):
    load = [
        pltpu.make_async_copy(pivot_ref, pivot, sems.at[0]),
        pltpu.make_async_copy(y_high_ref, y_high, sems.at[1]),
        pltpu.make_async_copy(y_low_ref, y_low, sems.at[2]),
    ]
    for copy in load:
        copy.start()
    for copy in load:
        copy.wait()
    chunk = 128

    def errors(index, _):
        first = pl.multiple_of(index * chunk, chunk)
        block = pl.ds(first, chunk)
        product = dot3(split(pivot[block]), (y_high[...], y_low[...]))
        row_ids = lax.broadcasted_iota(jnp.int32, (chunk, B), 0) + first
        col_ids = lax.broadcasted_iota(jnp.int32, (chunk, B), 1)
        high[block], low[block] = split(jnp.where(row_ids == col_ids, 1.0, 0.0) - product)
        return 0

    def squares(index, _):
        block = pl.ds(pl.multiple_of(index * chunk, chunk), chunk)
        other_high[block], other_low[block] = split(dot3((high[block], low[block]), (high[...], low[...])))
        base = y_high[block].astype(jnp.float32) + y_low[block].astype(jnp.float32)
        result[block] = base + dot3((y_high[block], y_low[block]), (high[...], low[...]))
        return 0

    def inverses(index, _):
        block = pl.ds(pl.multiple_of(index * chunk, chunk), chunk)
        base = result[block]
        high[block], low[block] = split(base + dot3(split(base), (other_high[...], other_low[...])))
        return 0

    lax.fori_loop(0, B // chunk, errors, 0)
    lax.fori_loop(0, B // chunk, squares, 0)
    lax.fori_loop(0, B // chunk, inverses, 0)
    store = [pltpu.make_async_copy(high, high_ref, sems.at[0]), pltpu.make_async_copy(low, low_ref, sems.at[1])]
    for copy in store:
        copy.start()
    for copy in store:
        copy.wait()


def multiply_kernel(owner, factors_in, cur_in, upper_in, received, high_ref, low_ref, factors, cur, front,
                    upper, multipliers, below, high, low, upper_high, upper_low, sems):
    rows = pl.ds((owner + 1) * SHARE, TALL)
    load = [
        pltpu.make_async_copy(factors_in.at[rows], below, sems.at[0]),
        pltpu.make_async_copy(high_ref, high, sems.at[1]),
        pltpu.make_async_copy(low_ref, low, sems.at[2]),
    ]
    if owner:
        load += [
            pltpu.make_async_copy(upper_in, upper, sems.at[3]),
            pltpu.make_async_copy(received, multipliers, sems.at[4]),
        ]
    for copy in load:
        copy.start()
    if owner:
        load[3].wait()
        split_into(upper, upper_high, upper_low)
    for copy in load[:3] + load[4:]:
        copy.wait()
    if owner:
        chunk = (TALL - SHARE) // 2

        def subtract(index, _):
            first = pl.multiple_of(index * chunk, 32)
            block = pl.ds(first, chunk)
            shifted = pl.ds(pl.multiple_of(first + SHARE, 32), chunk)
            below[block] = below[block] - dot3(split(multipliers[shifted]), (upper_high[...], upper_low[...]))
            return 0

        lax.fori_loop(0, 2, subtract, 0)
    part = 128

    def multiply(index, _):
        block = pl.ds(pl.multiple_of(index * part, part), part)
        below[block] = dot3(split(below[block]), (high[...], low[...]))
        return 0

    lax.fori_loop(0, TALL // part, multiply, 0)
    store = [
        pltpu.make_async_copy(below.at[pl.ds(0, SHARE)], front, sems.at[0]),
        pltpu.make_async_copy(below, cur, sems.at[1]),
        pltpu.make_async_copy(below, factors.at[rows], sems.at[2]),
    ]
    for copy in store:
        copy.start()
    for copy in store:
        copy.wait()


def front_kernel(step, factors_in, upper_in, received, following, upper, multipliers, target, high, low, sems):
    rows = pl.ds((step + 1) * SHARE, SHARE)
    load = [
        pltpu.make_async_copy(upper_in, upper, sems.at[0]),
        pltpu.make_async_copy(received, multipliers, sems.at[1]),
        pltpu.make_async_copy(factors_in.at[rows], target, sems.at[2]),
    ]
    for copy in load:
        copy.start()
    for copy in load:
        copy.wait()
    left = split(multipliers[...])
    split_into(upper, high, low)
    target[...] = target[...] - dot3(left, (high[...], low[...]))
    store = pltpu.make_async_copy(target, following, sems.at[0])
    store.start()
    store.wait()


def lag_of(step, table, panel):
    lag = jnp.int32(0)
    for distance, (amount, _) in table.items():
        if amount:
            lag = jnp.where(panel == step + distance, amount, lag)
    return lag


def update_kernel(step, far, scal, factors_in, cur_in, upper_in, received, factors, cur, following,
                  upper, multipliers, target, high, low, sems):
    panel = scal[0]
    source = step - lag_of(step, FAR if far else NEAR, panel)
    rows = pl.ds(pl.multiple_of((source + 1) * SHARE, SHARE), TALL)
    load = [
        pltpu.make_async_copy(upper_in, upper, sems.at[0]),
        pltpu.make_async_copy(received, multipliers, sems.at[1]),
        pltpu.make_async_copy(factors_in.at[rows], target, sems.at[2]),
    ]
    for copy in load:
        copy.start()
    load[0].wait()
    split_into(upper, high, low)
    load[1].wait()
    if far:
        keep = pltpu.make_async_copy(multipliers, cur, sems.at[3])
        keep.start()
    load[2].wait()
    chunk = 128

    def subtract(index, _):
        block = pl.ds(pl.multiple_of(index * chunk, chunk), chunk)
        target[block] = target[block] - dot3(split(multipliers[block]), (high[...], low[...]))
        return 0

    lax.fori_loop(0, TALL // chunk, subtract, 0)
    head = pl.ds(0, SHARE)
    tail = pl.ds(SHARE, TALL - SHARE)
    after = pl.ds(pl.multiple_of((source + 2) * SHARE, SHARE), TALL - SHARE)

    def put_head():
        first = pl.ds(pl.multiple_of((source + 1) * SHARE, SHARE), SHARE)
        store = [
            pltpu.make_async_copy(target.at[head], following, sems.at[0]),
            pltpu.make_async_copy(target.at[head], factors.at[first], sems.at[2]),
        ]
        for copy in store:
            copy.start()
        for copy in store:
            copy.wait()

    rest = pltpu.make_async_copy(target.at[tail], factors.at[after], sems.at[1])
    rest.start()
    if far:
        pl.when(panel != step + 2)(put_head)
        keep.wait()
    else:
        put_head()
    rest.wait()


def place_kernel(scal, factors_in, upper_in, pivot_ref, *rest):
    del upper_in
    parts, (factors, upper_out), (upper, swapped, picks, sems) = rest[:8], rest[8:10], rest[10:]
    place = scal[1]
    source = scal[2]
    z = place // 2
    core = place % 2
    load = []
    for index, part in enumerate(parts):
        other = core if index < 4 else 1 - core
        offset = (2 * ((z + 4 - index % 4) % 4) + other) * SHARE
        load.append(pltpu.make_async_copy(part, upper.at[pl.ds(pl.multiple_of(offset, SHARE), SHARE)], sems.at[index]))
    load.append(pltpu.make_async_copy(pivot_ref.at[source], picks, sems.at[8]))
    for copy in load:
        copy.start()
    for copy in load:
        copy.wait()
    keep = pltpu.make_async_copy(upper, upper_out, sems.at[0])
    keep.start()
    lanes = lax.broadcasted_iota(jnp.int32, (SHARE, 128), 1)
    swapped[...] = jnp.zeros_like(swapped)

    def pick_rows(group, _):
        onehot = jnp.where(picks[...] == lanes + 128 * group, 1.0, 0.0).astype(jnp.bfloat16)
        block = pl.ds(pl.multiple_of(group * 128, 128), 128)
        swapped[...] = swapped[...] + exact_rows(onehot, upper[block])
        return 0

    lax.fori_loop(0, B // 128, pick_rows, 0)
    at = pl.ds(pl.multiple_of(source * SHARE, SHARE), SHARE)
    store = pltpu.make_async_copy(swapped, factors.at[at], sems.at[1])
    store.start()
    store.wait()
    keep.wait()


ANY = pl.BlockSpec(memory_space=pl.ANY)
SMEM = pl.BlockSpec(memory_space=pltpu.SMEM)


def f32(*shape):
    return pltpu.VMEM(shape, jnp.float32)


def b16(*shape):
    return pltpu.VMEM(shape, jnp.bfloat16)


def like(*arrays):
    return [jax.ShapeDtypeStruct(a.shape, a.dtype) for a in arrays]


def call(kernel, out_shape, scratch, aliases, *operands, scal=None):
    first = [] if scal is None else [scal]
    return pl.pallas_call(
        kernel,
        out_shape=out_shape,
        in_specs=[SMEM] * len(first) + [ANY] * len(operands),
        out_specs=[ANY] * len(out_shape),
        scratch_shapes=scratch,
        input_output_aliases=aliases,
        compiler_params=pltpu.CompilerParams(vmem_limit_bytes=48 << 20),
    )(*first, *operands)


def inverse(pivot, y_high, y_low):
    scratch = [f32(B, B)] + [b16(B, B)] * 6 + [f32(B, B), pltpu.SemaphoreType.DMA((3,))]
    return call(inverse_kernel, like(y_high, y_low), scratch, {}, pivot, y_high, y_low)


def multiply(owner, factors, cur, front, upper, received, high, low):
    scratch = [f32(B, B), f32(TALL, B), f32(TALL, B)] + [b16(B, B)] * 4 + [pltpu.SemaphoreType.DMA((5,))]
    return call(functools.partial(multiply_kernel, owner), like(factors, cur, front), scratch, {0: 0, 1: 1},
                factors, cur, upper, received, high, low)


def advance(step, factors, following, upper, received):
    scratch = [f32(B, B), f32(SHARE, B), f32(SHARE, B), b16(B, B), b16(B, B), pltpu.SemaphoreType.DMA((3,))]
    return call(functools.partial(front_kernel, step), like(following), scratch, {}, factors, upper, received)[0]


def update(step, far, scal, factors, cur, following, upper, received):
    scratch = [f32(B, B), f32(TALL, B), f32(TALL, B), b16(B, B), b16(B, B), pltpu.SemaphoreType.DMA((4,))]
    outs = like(factors, cur, following) if far else like(factors, following)
    kernel = functools.partial(update_kernel if far else near_kernel, step, far)
    return call(kernel, outs, scratch, {1: 0, 2: 1} if far else {1: 0}, factors, cur, upper, received, scal=scal) if far else call(
        kernel, outs, scratch, {1: 0}, factors, upper, received, scal=scal)


def near_kernel(step, far, scal, factors_in, upper_in, received, factors, following, *scratch):
    update_kernel(step, far, scal, factors_in, None, upper_in, received, factors, None, following, *scratch)


def put_in_place(scal, factors, upper, picks, parts):
    scratch = [f32(B, B), f32(SHARE, B), pltpu.VMEM((SHARE, 128), jnp.int32), pltpu.SemaphoreType.DMA((9,))]
    return call(place_kernel, like(factors, upper), scratch, {1: 0, 2: 1}, factors, upper, picks, *parts, scal=scal)


def gather(share):
    swap = [(r, r ^ 1) for r in range(ROWS)]
    turned = [lax.ppermute(share, "row", [(r, (r + 2 * turn) % ROWS) for r in range(ROWS)]) for turn in (1, 2, 3)]
    beside = lax.ppermute(share, "row", swap)
    *turned, beside = lax.optimization_barrier((*turned, beside))
    return [share, *turned, beside] + [lax.ppermute(part, "row", swap) for part in turned]


def send(cur, step, table):
    first = step % TILE - TILE
    pairs = []
    for at in range(first, PANELS + TILE, TILE):
        for distance, (_, sender) in table.items():
            if at + sender in range(PANELS) and at + distance in range(PANELS):
                pairs += [((at + sender) * ROWS + r, (at + distance) * ROWS + r) for r in range(ROWS)]
    return lax.ppermute(cur, ("col", "row"), pairs)


def members(step, tables):
    takers = sorted({
        step + d for table in tables for d, (lag, _) in table.items() if step - lag >= 0 and step + d < PANELS
    })
    inside = set(takers)
    grown = True
    while grown:
        grown = False
        for table in tables:
            for distance, (_, sender) in table.items():
                pair = {step + sender, step + distance}
                if pair <= set(range(PANELS)) and pair & inside and not pair <= inside:
                    inside |= pair
                    grown = True
    return takers, sorted(inside)


def shifted(amount, group):
    return [
        (c * ROWS + r, (c + amount) * ROWS + r)
        for c in range(PANELS - amount) if c // amount % 2 == group for r in range(ROWS)
    ]


def among(panel, panels):
    hit = panel == panels[0]
    for other in panels[1:]:
        hit = hit | (panel == other)
    return hit


def local(matrix, pivots, seeds):
    panel = lax.axis_index("col").astype(jnp.int32)
    place = lax.axis_index("row").astype(jnp.int32)
    factors = matrix.reshape(-1, B)
    own_pivots = lax.dynamic_index_in_dim(pivots, panel, 0, keepdims=False)
    onehot = (own_pivots[:, None] == jnp.arange(B, dtype=jnp.int32)[None, :]).astype(jnp.float32)
    start = jnp.dot(seeds[0], onehot, precision=lax.Precision.HIGHEST, preferred_element_type=jnp.float32)
    half = jax.ShapeDtypeStruct((B, B), jnp.bfloat16)
    y_high, y_low = call(halves_kernel, [half, half], [f32(B, B), b16(B, B), b16(B, B), pltpu.SemaphoreType.DMA((2,))], {}, start)
    picks = jnp.broadcast_to(
        lax.dynamic_slice_in_dim(pivots, place * SHARE, SHARE, 1)[:, :, None], (PANELS, SHARE, 128)
    )
    first = jnp.maximum(panel - HB, 0)
    following = lax.dynamic_slice_in_dim(factors, first * SHARE, SHARE, 0)
    cur = jnp.zeros((TALL, B), jnp.float32)
    front = jnp.zeros((SHARE, B), jnp.float32)
    where = jnp.stack([panel, place])

    def when(panels, run, *state):
        if not panels:
            return state
        return lax.cond(among(panel, panels), lambda *state: tuple(run(*state)), lambda *state: state, *state)

    def collect(source, factors, upper, following):
        return put_in_place(jnp.stack([panel, place, source]), factors, upper, picks, gather(following))

    upper = jnp.zeros((B, B), jnp.float32)
    fresh = jnp.zeros((B, B), jnp.float32)

    def prepare(factors, upper):
        return collect(0, factors, upper, following)

    factors, upper = when([0, 1], prepare, factors, upper)

    def begin(factors, cur, front):
        return multiply(0, factors, cur, front, upper, cur, *inverse(upper, y_high, y_low))

    factors, cur, front = when([0], begin, factors, cur, front)

    for step in range(PANELS - 1):
        coming = step + 1

        def lead(following):
            arrived = lax.ppermute(front, ("col", "row"), shifted(1, step % 2))
            return (advance(step, factors, following, upper, arrived),)

        (following,) = when([step, coming], lead, following)
        near, _ = members(step, [NEAR])
        far, _ = members(step, [FAR])
        _, inside = members(step, [NEAR, FAR])

        def exchange(factors, cur, front, upper, fresh, following):
            p = send(cur, step, NEAR)
            q = send(cur, step, FAR) if far else None
            source = jnp.where(
                panel == coming, coming, jnp.maximum(step - lag_of(step, FAR | NEAR, panel), 0)
            )

            def bring(factors, fresh):
                return collect(source, factors, fresh, following)

            factors, fresh = when(sorted(set(near) | set(far)), bring, factors, fresh)
            high, low = inverse(fresh, y_high, y_low)

            def near_update(factors, following):
                return update(step, False, where, factors, cur, following, fresh, p)

            factors, following = when([c for c in near if c != coming], near_update, factors, following)

            def again(factors, fresh):
                return collect(step + 1 - lag_of(step, NEAR, panel), factors, fresh, following)

            factors, fresh = when(sorted(set(near) & set(far)), again, factors, fresh)
            if far:
                def second(following):
                    arrived = lax.ppermute(front, ("col", "row"), shifted(2, step // 2 % 2))
                    return (advance(step, factors, following, fresh, arrived),)

                (following,) = when([step, step + 2], second, following)

                def ahead(factors, upper):
                    return collect(coming, factors, upper, following)

                factors, upper = when([step + 2], ahead, factors, upper)

            def far_update(factors, cur, following):
                return update(step, True, where, factors, cur, following, fresh, q)

            factors, cur, following = when(far, far_update, factors, cur, following)

            def own(factors, cur, front):
                return multiply(coming, factors, cur, front, upper, p, high, low)

            factors, cur, front = when([coming], own, factors, cur, front)
            return factors, cur, front, upper, fresh, following

        factors, cur, front, upper, fresh, following = when(
            inside, exchange, factors, cur, front, upper, fresh, following
        )
    at = (panel + 1) * SHARE
    own = lax.dynamic_slice_in_dim(factors, at, TALL, 0)
    own = lax.dot_general(
        own, onehot, (((1,), (1,)), ((), ())), precision=lax.Precision.HIGHEST, preferred_element_type=jnp.float32
    )
    factors = lax.dynamic_update_slice_in_dim(factors, own, at, 0)
    return factors.reshape(matrix.shape)


def solution(mesh):
    return jax.shard_map(
        local,
        mesh=mesh,
        in_specs=(P(None, "row", "col"), P(), P("col", None, None)),
        out_specs=P(None, "row", "col"),
        check_vma=False,
    )
```

```python
import functools

import jax
import jax.numpy as jnp
from jax import lax
from jax.experimental import pallas as pl
from jax.experimental.pallas import tpu as pltpu
from jax.sharding import PartitionSpec as P

HB = 8
PANELS = 16
B = 512
ROWS = 8
SHARE = B // ROWS
TALL = HB * SHARE
TILE = 9

NEAR = {2: (1, -1), 3: (2, -2), 4: (2, 2)}
FAR = {2: (0, 0), 3: (1, -1), 5: (2, -2), 6: (2, 2)}


def split(value):
    high = value.astype(jnp.bfloat16)
    low = (value - high.astype(jnp.float32)).astype(jnp.bfloat16)
    return high, low


def dot(left, right):
    return jnp.dot(left, right, preferred_element_type=jnp.float32)


def dot3(left, right):
    return dot(left[0], right[0]) + (dot(left[0], right[1]) + dot(left[1], right[0]))


def exact_rows(onehot, value):
    high = value.astype(jnp.bfloat16)
    rest = value - high.astype(jnp.float32)
    mid = rest.astype(jnp.bfloat16)
    low = (rest - mid.astype(jnp.float32)).astype(jnp.bfloat16)
    return dot(onehot, high) + (dot(onehot, mid) + dot(onehot, low))


def split_into(value, high, low):
    def rows(index, _):
        block = pl.ds(pl.multiple_of(index * SHARE, SHARE), SHARE)
        high[block], low[block] = split(value[block])
        return 0

    lax.fori_loop(0, B // SHARE, rows, 0)


def halves_kernel(value_ref, high_ref, low_ref, value, high, low, sems):
    load = pltpu.make_async_copy(value_ref, value, sems.at[0])
    load.start()
    load.wait()
    split_into(value, high, low)
    store = [pltpu.make_async_copy(high, high_ref, sems.at[0]), pltpu.make_async_copy(low, low_ref, sems.at[1])]
    for copy in store:
        copy.start()
    for copy in store:
        copy.wait()


def inverse_kernel(owner, pivot_ref, y_high_ref, y_low_ref, high_ref, low_ref,
                   pivot, y_high, y_low, high, low, other_high, other_low, result, sems):
    load = [
        pltpu.make_async_copy(pivot_ref.at[pl.ds(owner % 2 * B, B)], pivot, sems.at[0]),
        pltpu.make_async_copy(y_high_ref, y_high, sems.at[1]),
        pltpu.make_async_copy(y_low_ref, y_low, sems.at[2]),
    ]
    for copy in load:
        copy.start()
    for copy in load:
        copy.wait()
    chunk = 128

    def errors(index, _):
        first = pl.multiple_of(index * chunk, chunk)
        block = pl.ds(first, chunk)
        product = dot3(split(pivot[block]), (y_high[...], y_low[...]))
        row_ids = lax.broadcasted_iota(jnp.int32, (chunk, B), 0) + first
        col_ids = lax.broadcasted_iota(jnp.int32, (chunk, B), 1)
        high[block], low[block] = split(jnp.where(row_ids == col_ids, 1.0, 0.0) - product)
        return 0

    def squares(index, _):
        block = pl.ds(pl.multiple_of(index * chunk, chunk), chunk)
        other_high[block], other_low[block] = split(dot3((high[block], low[block]), (high[...], low[...])))
        base = y_high[block].astype(jnp.float32) + y_low[block].astype(jnp.float32)
        result[block] = base + dot3((y_high[block], y_low[block]), (high[...], low[...]))
        return 0

    def inverses(index, _):
        block = pl.ds(pl.multiple_of(index * chunk, chunk), chunk)
        base = result[block]
        high[block], low[block] = split(base + dot3(split(base), (other_high[...], other_low[...])))
        return 0

    lax.fori_loop(0, B // chunk, errors, 0)
    lax.fori_loop(0, B // chunk, squares, 0)
    lax.fori_loop(0, B // chunk, inverses, 0)
    store = [pltpu.make_async_copy(high, high_ref, sems.at[0]), pltpu.make_async_copy(low, low_ref, sems.at[1])]
    for copy in store:
        copy.start()
    for copy in store:
        copy.wait()


def multiply_kernel(owner, factors_in, cur_in, upper_in, received, high_ref, low_ref, factors, cur, front,
                    upper, multipliers, below, high, low, upper_high, upper_low, sems):
    rows = pl.ds((owner + 1) * SHARE, TALL)
    load = [
        pltpu.make_async_copy(factors_in.at[rows], below, sems.at[0]),
        pltpu.make_async_copy(high_ref, high, sems.at[1]),
        pltpu.make_async_copy(low_ref, low, sems.at[2]),
    ]
    if owner:
        load += [
            pltpu.make_async_copy(upper_in.at[pl.ds((owner - 1) % 2 * B, B)], upper, sems.at[3]),
            pltpu.make_async_copy(received, multipliers, sems.at[4]),
        ]
    for copy in load:
        copy.start()
    if owner:
        load[3].wait()
        split_into(upper, upper_high, upper_low)
    for copy in load[:3] + load[4:]:
        copy.wait()
    if owner:
        chunk = (TALL - SHARE) // 2

        def subtract(index, _):
            first = pl.multiple_of(index * chunk, 32)
            block = pl.ds(first, chunk)
            shifted = pl.ds(pl.multiple_of(first + SHARE, 32), chunk)
            below[block] = below[block] - dot3(split(multipliers[shifted]), (upper_high[...], upper_low[...]))
            return 0

        lax.fori_loop(0, 2, subtract, 0)
    part = 128

    def multiply(index, _):
        block = pl.ds(pl.multiple_of(index * part, part), part)
        below[block] = dot3(split(below[block]), (high[...], low[...]))
        return 0

    lax.fori_loop(0, TALL // part, multiply, 0)
    store = [
        pltpu.make_async_copy(below.at[pl.ds(0, SHARE)], front, sems.at[0]),
        pltpu.make_async_copy(below, cur, sems.at[1]),
        pltpu.make_async_copy(below, factors.at[rows], sems.at[2]),
    ]
    for copy in store:
        copy.start()
    for copy in store:
        copy.wait()


def front_kernel(step, factors_in, upper_in, received, following, upper, multipliers, target, high, low, sems):
    rows = pl.ds((step + 1) * SHARE, SHARE)
    load = [
        pltpu.make_async_copy(upper_in.at[pl.ds(step % 2 * B, B)], upper, sems.at[0]),
        pltpu.make_async_copy(received, multipliers, sems.at[1]),
        pltpu.make_async_copy(factors_in.at[rows], target, sems.at[2]),
    ]
    for copy in load:
        copy.start()
    for copy in load:
        copy.wait()
    left = split(multipliers[...])
    split_into(upper, high, low)
    target[...] = target[...] - dot3(left, (high[...], low[...]))
    store = pltpu.make_async_copy(target, following, sems.at[0])
    store.start()
    store.wait()


def lag_of(step, table, panel):
    lag = jnp.int32(0)
    for distance, (amount, _) in table.items():
        if amount:
            lag = jnp.where(panel == step + distance, amount, lag)
    return lag


def update_kernel(step, far, scal, factors_in, cur_in, following_in, upper_in, received, factors, cur, following,
                  upper, multipliers, target, high, low, sems):
    panel = scal[0]
    table = FAR if far else NEAR
    source = step - lag_of(step, table, panel)
    takes = jnp.bool_(False)
    for distance, (amount, _) in table.items():
        if step - amount >= 0:
            takes = takes | (panel == step + distance)

    @pl.when(takes)
    def _():
        rows = pl.ds(pl.multiple_of((source + 1) * SHARE, SHARE), TALL)
        slot = pl.ds(pl.multiple_of(lax.rem(source, 2) * B, B), B)
        load = [
            pltpu.make_async_copy(upper_in.at[slot], upper, sems.at[0]),
            pltpu.make_async_copy(received, multipliers, sems.at[1]),
            pltpu.make_async_copy(factors_in.at[rows], target, sems.at[2]),
        ]
        for copy in load:
            copy.start()
        load[0].wait()
        split_into(upper, high, low)
        load[1].wait()
        if far:
            keep = pltpu.make_async_copy(multipliers, cur, sems.at[3])
            keep.start()
        load[2].wait()
        chunk = 128

        def subtract(index, _):
            block = pl.ds(pl.multiple_of(index * chunk, chunk), chunk)
            target[block] = target[block] - dot3(split(multipliers[block]), (high[...], low[...]))
            return 0

        lax.fori_loop(0, TALL // chunk, subtract, 0)
        head = pl.ds(0, SHARE)
        tail = pl.ds(SHARE, TALL - SHARE)
        after = pl.ds(pl.multiple_of((source + 2) * SHARE, SHARE), TALL - SHARE)

        def put_head():
            first = pl.ds(pl.multiple_of((source + 1) * SHARE, SHARE), SHARE)
            store = [
                pltpu.make_async_copy(target.at[head], following, sems.at[0]),
                pltpu.make_async_copy(target.at[head], factors.at[first], sems.at[2]),
            ]
            for copy in store:
                copy.start()
            for copy in store:
                copy.wait()

        rest = pltpu.make_async_copy(target.at[tail], factors.at[after], sems.at[1])
        rest.start()
        if far:
            pl.when(panel != step + 2)(put_head)
            keep.wait()
        else:
            put_head()
        rest.wait()


def place_kernel(scal, factors_in, upper_in, pivot_ref, *rest):
    del upper_in
    parts, (factors, upper_out), (upper, swapped, picks, sems) = rest[:8], rest[8:10], rest[10:]
    place = scal[1]
    source = scal[2]
    z = place // 2
    core = place % 2
    load = []
    for index, part in enumerate(parts):
        other = core if index < 4 else 1 - core
        offset = (2 * ((z + 4 - index % 4) % 4) + other) * SHARE
        load.append(pltpu.make_async_copy(part, upper.at[pl.ds(pl.multiple_of(offset, SHARE), SHARE)], sems.at[index]))
    load.append(pltpu.make_async_copy(pivot_ref.at[source], picks, sems.at[8]))
    for copy in load:
        copy.start()
    for copy in load:
        copy.wait()
    slot = pl.ds(pl.multiple_of(lax.rem(source, 2) * B, B), B)
    keep = pltpu.make_async_copy(upper, upper_out.at[slot], sems.at[0])
    keep.start()
    lanes = lax.broadcasted_iota(jnp.int32, (SHARE, 128), 1)
    swapped[...] = jnp.zeros_like(swapped)

    def pick_rows(group, _):
        onehot = jnp.where(picks[...] == lanes + 128 * group, 1.0, 0.0).astype(jnp.bfloat16)
        block = pl.ds(pl.multiple_of(group * 128, 128), 128)
        swapped[...] = swapped[...] + exact_rows(onehot, upper[block])
        return 0

    lax.fori_loop(0, B // 128, pick_rows, 0)
    at = pl.ds(pl.multiple_of(source * SHARE, SHARE), SHARE)
    store = pltpu.make_async_copy(swapped, factors.at[at], sems.at[1])
    store.start()
    store.wait()
    keep.wait()


ANY = pl.BlockSpec(memory_space=pl.ANY)
SMEM = pl.BlockSpec(memory_space=pltpu.SMEM)


def f32(*shape):
    return pltpu.VMEM(shape, jnp.float32)


def b16(*shape):
    return pltpu.VMEM(shape, jnp.bfloat16)


def like(*arrays):
    return [jax.ShapeDtypeStruct(a.shape, a.dtype) for a in arrays]


def call(kernel, out_shape, scratch, aliases, *operands, scal=None):
    first = [] if scal is None else [scal]
    return pl.pallas_call(
        kernel,
        out_shape=out_shape,
        in_specs=[SMEM] * len(first) + [ANY] * len(operands),
        out_specs=[ANY] * len(out_shape),
        scratch_shapes=scratch,
        input_output_aliases=aliases,
        compiler_params=pltpu.CompilerParams(vmem_limit_bytes=48 << 20),
    )(*first, *operands)


def inverse(owner, pivot, y_high, y_low):
    scratch = [f32(B, B)] + [b16(B, B)] * 6 + [f32(B, B), pltpu.SemaphoreType.DMA((3,))]
    return call(functools.partial(inverse_kernel, owner), like(y_high, y_low), scratch, {}, pivot, y_high, y_low)


def multiply(owner, factors, cur, front, upper, received, high, low):
    scratch = [f32(B, B), f32(TALL, B), f32(TALL, B)] + [b16(B, B)] * 4 + [pltpu.SemaphoreType.DMA((5,))]
    return call(functools.partial(multiply_kernel, owner), like(factors, cur, front), scratch, {0: 0, 1: 1},
                factors, cur, upper, received, high, low)


def advance(step, factors, following, upper, received):
    scratch = [f32(B, B), f32(SHARE, B), f32(SHARE, B), b16(B, B), b16(B, B), pltpu.SemaphoreType.DMA((3,))]
    return call(functools.partial(front_kernel, step), like(following), scratch, {}, factors, upper, received)[0]


def near_kernel(step, far, scal, factors_in, following_in, upper_in, received, factors, following, *scratch):
    update_kernel(step, far, scal, factors_in, None, following_in, upper_in, received, factors, None, following, *scratch)


def update(step, far, scal, factors, cur, following, upper, received):
    scratch = [f32(B, B), f32(TALL, B), f32(TALL, B), b16(B, B), b16(B, B), pltpu.SemaphoreType.DMA((4,))]
    if far:
        return call(functools.partial(update_kernel, step, far), like(factors, cur, following), scratch,
                    {1: 0, 2: 1, 3: 2}, factors, cur, following, upper, received, scal=scal)
    return call(functools.partial(near_kernel, step, far), like(factors, following), scratch,
                {1: 0, 2: 1}, factors, following, upper, received, scal=scal)


def put_in_place(scal, factors, upper, picks, parts):
    scratch = [f32(B, B), f32(SHARE, B), pltpu.VMEM((SHARE, 128), jnp.int32), pltpu.SemaphoreType.DMA((9,))]
    return call(place_kernel, like(factors, upper), scratch, {1: 0, 2: 1}, factors, upper, picks, *parts, scal=scal)


def gather(share):
    swap = [(r, r ^ 1) for r in range(ROWS)]
    turned = [lax.ppermute(share, "row", [(r, (r + 2 * turn) % ROWS) for r in range(ROWS)]) for turn in (1, 2, 3)]
    beside = lax.ppermute(share, "row", swap)
    *turned, beside = lax.optimization_barrier((*turned, beside))
    return [share, *turned, beside] + [lax.ppermute(part, "row", swap) for part in turned]


def send(cur, step, table):
    first = step % TILE - TILE
    pairs = []
    for at in range(first, PANELS + TILE, TILE):
        for distance, (_, sender) in table.items():
            if at + sender in range(PANELS) and at + distance in range(PANELS):
                pairs += [((at + sender) * ROWS + r, (at + distance) * ROWS + r) for r in range(ROWS)]
    return lax.ppermute(cur, ("col", "row"), pairs)


def members(step, tables):
    takers = sorted({
        step + d for table in tables for d, (lag, _) in table.items() if step - lag >= 0 and step + d < PANELS
    })
    inside = set(takers)
    grown = True
    while grown:
        grown = False
        for table in tables:
            for distance, (_, sender) in table.items():
                pair = {step + sender, step + distance}
                if pair <= set(range(PANELS)) and pair & inside and not pair <= inside:
                    inside |= pair
                    grown = True
    return takers, sorted(inside)


def shifted(amount, group):
    return [
        (c * ROWS + r, (c + amount) * ROWS + r)
        for c in range(PANELS - amount) if c // amount % 2 == group for r in range(ROWS)
    ]


def among(panel, panels):
    hit = panel == panels[0]
    for other in panels[1:]:
        hit = hit | (panel == other)
    return hit


def local(matrix, pivots, seeds):
    panel = lax.axis_index("col").astype(jnp.int32)
    place = lax.axis_index("row").astype(jnp.int32)
    factors = matrix.reshape(-1, B)
    own_pivots = lax.dynamic_index_in_dim(pivots, panel, 0, keepdims=False)
    onehot = (own_pivots[:, None] == jnp.arange(B, dtype=jnp.int32)[None, :]).astype(jnp.float32)
    start = jnp.dot(seeds[0], onehot, precision=lax.Precision.HIGHEST, preferred_element_type=jnp.float32)
    half = jax.ShapeDtypeStruct((B, B), jnp.bfloat16)
    y_high, y_low = call(halves_kernel, [half, half], [f32(B, B), b16(B, B), b16(B, B), pltpu.SemaphoreType.DMA((2,))], {}, start)
    picks = jnp.broadcast_to(
        lax.dynamic_slice_in_dim(pivots, place * SHARE, SHARE, 1)[:, :, None], (PANELS, SHARE, 128)
    )
    first = jnp.maximum(panel - HB, 0)
    following = lax.dynamic_slice_in_dim(factors, first * SHARE, SHARE, 0)
    cur = jnp.zeros((TALL, B), jnp.float32)
    front = jnp.zeros((SHARE, B), jnp.float32)
    where = jnp.stack([panel, place])

    def when(panels, run, *state):
        if not panels:
            return state
        return lax.cond(among(panel, panels), lambda *state: tuple(run(*state)), lambda *state: state, *state)

    def collect(source, factors, upper, following):
        return put_in_place(jnp.stack([panel, place, source]), factors, upper, picks, gather(following))

    upper = jnp.zeros((2 * B, B), jnp.float32)

    def prepare(factors, upper):
        return collect(0, factors, upper, following)

    factors, upper = when([0, 1, 2], prepare, factors, upper)

    def begin(factors, cur, front):
        return multiply(0, factors, cur, front, upper, cur, *inverse(0, upper, y_high, y_low))

    factors, cur, front = when([0], begin, factors, cur, front)

    high, low = y_high, y_low
    bulk = jnp.zeros((TALL, B), jnp.float32)
    for step in range(PANELS - 1):
        coming = step + 1
        near, near_inside = members(step, [NEAR])
        far, far_inside = members(step, [FAR])

        def approach(factors, upper, following):
            p = send(cur, step, NEAR)
            source = step - lag_of(step, NEAR, panel)

            def bring(factors, upper):
                return collect(source, factors, upper, following)

            factors, upper = when(near, bring, factors, upper)
            factors, following = update(step, False, where, factors, cur, following, upper, p)

            def again(factors, upper):
                return collect(source + 1, factors, upper, following)

            factors, upper = when(sorted(set(near) & set(far)), again, factors, upper)
            return factors, upper, following

        factors, upper, following = when(near_inside, approach, factors, upper, following)

        def lead(following):
            arrived = lax.ppermute(front, ("col", "row"), shifted(1, step % 2))
            return (advance(step, factors, following, upper, arrived),)

        (following,) = when([step, coming], lead, following)

        def second(following):
            arrived = lax.ppermute(front, ("col", "row"), shifted(2, step // 2 % 2))
            return (advance(step, factors, following, upper, arrived),)

        if far:
            (following,) = when([step, step + 2], second, following)

        def exchange(factors, cur, front, upper, following, bulk, high, low):
            q = send(cur, step, FAR) if far else None
            source = jnp.where(panel <= step + 2, coming, jnp.maximum(step - lag_of(step, FAR, panel), 0))

            def bring(factors, upper):
                return collect(source, factors, upper, following)

            factors, upper = when(sorted(set(far) - set(near) | set(far) & {step + 2} | {coming}), bring, factors, upper)

            def critical(bulk, high, low):
                bulk = lax.ppermute(cur, ("col", "row"), shifted(1, step % 2))
                high, low = inverse(coming, upper, y_high, y_low)
                return bulk, high, low

            bulk, high, low = when([step, coming], critical, bulk, high, low)
            if far:
                def far_update(factors, cur, following):
                    return update(step, True, where, factors, cur, following, upper, q)

                factors, cur, following = when(far, far_update, factors, cur, following)

            def own(factors, cur, front):
                return multiply(coming, factors, cur, front, upper, bulk, high, low)

            factors, cur, front = when([coming], own, factors, cur, front)
            return factors, cur, front, upper, following, bulk, high, low

        inside = sorted(set(far_inside) | {step, coming})
        factors, cur, front, upper, following, bulk, high, low = when(
            inside, exchange, factors, cur, front, upper, following, bulk, high, low
        )
    at = (panel + 1) * SHARE
    own = lax.dynamic_slice_in_dim(factors, at, TALL, 0)
    own = lax.dot_general(
        own, onehot, (((1,), (1,)), ((), ())), precision=lax.Precision.HIGHEST, preferred_element_type=jnp.float32
    )
    factors = lax.dynamic_update_slice_in_dim(factors, own, at, 0)
    return factors.reshape(matrix.shape)


def solution(mesh):
    return jax.shard_map(
        local,
        mesh=mesh,
        in_specs=(P(None, "row", "col"), P(), P("col", None, None)),
        out_specs=P(None, "row", "col"),
        check_vma=False,
    )
```

```python
import functools

import jax
import jax.numpy as jnp
from jax import lax
from jax.experimental import pallas as pl
from jax.experimental.pallas import tpu as pltpu
from jax.sharding import PartitionSpec as P

HB = 8
PANELS = 16
B = 512
ROWS = 8
SHARE = B // ROWS
TALL = HB * SHARE
TILE = 9

NEAR = {1: (0, 0), 2: (1, -1), 3: (2, -2), 4: (2, 2)}
FAR = {2: (0, 0), 3: (1, -1), 5: (2, -2), 6: (2, 2)}


def split(value):
    high = value.astype(jnp.bfloat16)
    low = (value - high.astype(jnp.float32)).astype(jnp.bfloat16)
    return high, low


def dot(left, right):
    return jnp.dot(left, right, preferred_element_type=jnp.float32)


def dot3(left, right):
    return dot(left[0], right[0]) + (dot(left[0], right[1]) + dot(left[1], right[0]))


def exact_rows(onehot, value):
    high = value.astype(jnp.bfloat16)
    rest = value - high.astype(jnp.float32)
    mid = rest.astype(jnp.bfloat16)
    low = (rest - mid.astype(jnp.float32)).astype(jnp.bfloat16)
    return dot(onehot, high) + (dot(onehot, mid) + dot(onehot, low))


def split_into(value, high, low):
    def rows(index, _):
        block = pl.ds(pl.multiple_of(index * SHARE, SHARE), SHARE)
        high[block], low[block] = split(value[block])
        return 0

    lax.fori_loop(0, B // SHARE, rows, 0)


def halves_kernel(value_ref, high_ref, low_ref, value, high, low, sems):
    load = pltpu.make_async_copy(value_ref, value, sems.at[0])
    load.start()
    load.wait()
    split_into(value, high, low)
    store = [pltpu.make_async_copy(high, high_ref, sems.at[0]), pltpu.make_async_copy(low, low_ref, sems.at[1])]
    for copy in store:
        copy.start()
    for copy in store:
        copy.wait()


def inverse_kernel(pivot_ref, y_high_ref, y_low_ref, high_ref, low_ref,
                   pivot, y_high, y_low, high, low, other_high, other_low, result, sems):
    load = [
        pltpu.make_async_copy(pivot_ref, pivot, sems.at[0]),
        pltpu.make_async_copy(y_high_ref, y_high, sems.at[1]),
        pltpu.make_async_copy(y_low_ref, y_low, sems.at[2]),
    ]
    for copy in load:
        copy.start()
    for copy in load:
        copy.wait()
    chunk = 128

    def errors(index, _):
        first = pl.multiple_of(index * chunk, chunk)
        block = pl.ds(first, chunk)
        product = dot3(split(pivot[block]), (y_high[...], y_low[...]))
        row_ids = lax.broadcasted_iota(jnp.int32, (chunk, B), 0) + first
        col_ids = lax.broadcasted_iota(jnp.int32, (chunk, B), 1)
        high[block], low[block] = split(jnp.where(row_ids == col_ids, 1.0, 0.0) - product)
        return 0

    def squares(index, _):
        block = pl.ds(pl.multiple_of(index * chunk, chunk), chunk)
        other_high[block], other_low[block] = split(dot3((high[block], low[block]), (high[...], low[...])))
        base = y_high[block].astype(jnp.float32) + y_low[block].astype(jnp.float32)
        result[block] = base + dot3((y_high[block], y_low[block]), (high[...], low[...]))
        return 0

    def inverses(index, _):
        block = pl.ds(pl.multiple_of(index * chunk, chunk), chunk)
        base = result[block]
        high[block], low[block] = split(base + dot3(split(base), (other_high[...], other_low[...])))
        return 0

    lax.fori_loop(0, B // chunk, errors, 0)
    lax.fori_loop(0, B // chunk, squares, 0)
    lax.fori_loop(0, B // chunk, inverses, 0)
    store = [pltpu.make_async_copy(high, high_ref, sems.at[0]), pltpu.make_async_copy(low, low_ref, sems.at[1])]
    for copy in store:
        copy.start()
    for copy in store:
        copy.wait()


def multiply_kernel(owner, factors_in, cur_in, upper_in, received, high_ref, low_ref, factors, cur, front,
                    upper, multipliers, below, high, low, upper_high, upper_low, sems):
    rows = pl.ds((owner + 1) * SHARE, TALL)
    load = [
        pltpu.make_async_copy(factors_in.at[rows], below, sems.at[0]),
        pltpu.make_async_copy(high_ref, high, sems.at[1]),
        pltpu.make_async_copy(low_ref, low, sems.at[2]),
    ]
    if owner:
        load += [
            pltpu.make_async_copy(upper_in, upper, sems.at[3]),
            pltpu.make_async_copy(received, multipliers, sems.at[4]),
        ]
    for copy in load:
        copy.start()
    if owner:
        load[3].wait()
        split_into(upper, upper_high, upper_low)
    for copy in load[:3] + load[4:]:
        copy.wait()
    if owner:
        chunk = (TALL - SHARE) // 2

        def subtract(index, _):
            first = pl.multiple_of(index * chunk, 32)
            block = pl.ds(first, chunk)
            shifted = pl.ds(pl.multiple_of(first + SHARE, 32), chunk)
            below[block] = below[block] - dot3(split(multipliers[shifted]), (upper_high[...], upper_low[...]))
            return 0

        lax.fori_loop(0, 2, subtract, 0)
    part = 128

    def multiply(index, _):
        block = pl.ds(pl.multiple_of(index * part, part), part)
        below[block] = dot3(split(below[block]), (high[...], low[...]))
        return 0

    lax.fori_loop(0, TALL // part, multiply, 0)
    store = [
        pltpu.make_async_copy(below.at[pl.ds(0, SHARE)], front, sems.at[0]),
        pltpu.make_async_copy(below, cur, sems.at[1]),
        pltpu.make_async_copy(below, factors.at[rows], sems.at[2]),
    ]
    for copy in store:
        copy.start()
    for copy in store:
        copy.wait()


def front_kernel(step, factors_in, upper_in, received, following, upper, multipliers, target, high, low, sems):
    rows = pl.ds((step + 1) * SHARE, SHARE)
    load = [
        pltpu.make_async_copy(upper_in, upper, sems.at[0]),
        pltpu.make_async_copy(received.at[pl.ds(0, SHARE)], multipliers, sems.at[1]),
        pltpu.make_async_copy(factors_in.at[rows], target, sems.at[2]),
    ]
    for copy in load:
        copy.start()
    for copy in load:
        copy.wait()
    left = split(multipliers[...])
    split_into(upper, high, low)
    target[...] = target[...] - dot3(left, (high[...], low[...]))
    store = pltpu.make_async_copy(target, following, sems.at[0])
    store.start()
    store.wait()


def lag_of(step, table, panel):
    lag = jnp.int32(0)
    for distance, (amount, _) in table.items():
        if amount:
            lag = jnp.where(panel == step + distance, amount, lag)
    return lag


def update_kernel(step, far, scal, factors_in, cur_in, upper_in, received, factors, cur, following,
                  upper, multipliers, target, high, low, sems):
    panel = scal[0]
    source = step - lag_of(step, FAR if far else NEAR, panel)
    rows = pl.ds(pl.multiple_of((source + 1) * SHARE, SHARE), TALL)
    load = [
        pltpu.make_async_copy(upper_in, upper, sems.at[0]),
        pltpu.make_async_copy(received, multipliers, sems.at[1]),
        pltpu.make_async_copy(factors_in.at[rows], target, sems.at[2]),
    ]
    for copy in load:
        copy.start()
    load[0].wait()
    split_into(upper, high, low)
    load[1].wait()
    if far:
        keep = pltpu.make_async_copy(multipliers, cur, sems.at[3])
        keep.start()
    load[2].wait()
    chunk = 128

    def subtract(index, _):
        block = pl.ds(pl.multiple_of(index * chunk, chunk), chunk)
        target[block] = target[block] - dot3(split(multipliers[block]), (high[...], low[...]))
        return 0

    lax.fori_loop(0, TALL // chunk, subtract, 0)
    head = pl.ds(0, SHARE)
    tail = pl.ds(SHARE, TALL - SHARE)
    after = pl.ds(pl.multiple_of((source + 2) * SHARE, SHARE), TALL - SHARE)

    def put_head():
        first = pl.ds(pl.multiple_of((source + 1) * SHARE, SHARE), SHARE)
        store = [
            pltpu.make_async_copy(target.at[head], following, sems.at[0]),
            pltpu.make_async_copy(target.at[head], factors.at[first], sems.at[2]),
        ]
        for copy in store:
            copy.start()
        for copy in store:
            copy.wait()

    rest = pltpu.make_async_copy(target.at[tail], factors.at[after], sems.at[1])
    rest.start()
    if far:
        pl.when(panel != step + 2)(put_head)
        keep.wait()
    else:
        put_head()
    rest.wait()


def place_kernel(scal, upper_in, *rest):
    parts, (upper_out, upper, sems) = rest[:8], rest[8:]
    del upper_in
    place = scal[1]
    z = place // 2
    core = place % 2
    load = []
    for index, part in enumerate(parts):
        other = core if index < 4 else 1 - core
        offset = (2 * ((z + 4 - index % 4) % 4) + other) * SHARE
        at = pl.ds(pl.multiple_of(offset, SHARE), SHARE)
        load.append(pltpu.make_async_copy(part, upper.at[at], sems.at[index]))
    for copy in load:
        copy.start()
    for copy in load:
        copy.wait()
    keep = pltpu.make_async_copy(upper, upper_out, sems.at[0])
    keep.start()
    keep.wait()


def swap_kernel(scal, factors_in, upper_in, pivot_ref, factors, upper, swapped, picks, sems):
    del factors_in
    source = scal[2]

    @pl.when(source >= 0)
    def _():
        load = [
            pltpu.make_async_copy(upper_in, upper, sems.at[0]),
            pltpu.make_async_copy(pivot_ref.at[source], picks, sems.at[1]),
        ]
        for copy in load:
            copy.start()
        for copy in load:
            copy.wait()
        lanes = lax.broadcasted_iota(jnp.int32, (SHARE, 128), 1)
        swapped[...] = jnp.zeros_like(swapped)

        def pick_rows(group, _):
            onehot = jnp.where(picks[...] == lanes + 128 * group, 1.0, 0.0).astype(jnp.bfloat16)
            block = pl.ds(pl.multiple_of(group * 128, 128), 128)
            swapped[...] = swapped[...] + exact_rows(onehot, upper[block])
            return 0

        lax.fori_loop(0, B // 128, pick_rows, 0)
        at = pl.ds(pl.multiple_of(source * SHARE, SHARE), SHARE)
        store = pltpu.make_async_copy(swapped, factors.at[at], sems.at[0])
        store.start()
        store.wait()


ANY = pl.BlockSpec(memory_space=pl.ANY)
SMEM = pl.BlockSpec(memory_space=pltpu.SMEM)
HBM = pl.BlockSpec(memory_space=pltpu.HBM)


def f32(*shape):
    return pltpu.VMEM(shape, jnp.float32)


def b16(*shape):
    return pltpu.VMEM(shape, jnp.bfloat16)


def like(*arrays):
    return [jax.ShapeDtypeStruct(a.shape, a.dtype) for a in arrays]


def space(array):
    return HBM if array.shape[0] > TALL else ANY


def call(kernel, out_shape, scratch, aliases, *operands, scal=None):
    first = [] if scal is None else [scal]
    return pl.pallas_call(
        kernel,
        out_shape=out_shape,
        in_specs=[SMEM] * len(first) + [space(a) for a in operands],
        out_specs=[space(a) for a in out_shape],
        scratch_shapes=scratch,
        input_output_aliases=aliases,
        compiler_params=pltpu.CompilerParams(vmem_limit_bytes=48 << 20),
    )(*first, *operands)


def inverse(pivot, y_high, y_low):
    scratch = [f32(B, B)] + [b16(B, B)] * 6 + [f32(B, B), pltpu.SemaphoreType.DMA((3,))]
    return call(inverse_kernel, like(y_high, y_low), scratch, {}, pivot, y_high, y_low)


def multiply(owner, factors, cur, front, upper, received, high, low):
    scratch = [f32(B, B), f32(TALL, B), f32(TALL, B)] + [b16(B, B)] * 4 + [pltpu.SemaphoreType.DMA((5,))]
    return call(functools.partial(multiply_kernel, owner), like(factors, cur, front), scratch, {0: 0, 1: 1},
                factors, cur, upper, received, high, low)


def advance(step, factors, following, upper, received):
    scratch = [f32(B, B), f32(SHARE, B), f32(SHARE, B), b16(B, B), b16(B, B), pltpu.SemaphoreType.DMA((3,))]
    return call(functools.partial(front_kernel, step), like(following), scratch, {}, factors, upper, received)[0]


def update(step, far, scal, factors, cur, following, upper, received):
    scratch = [f32(B, B), f32(TALL, B), f32(TALL, B), b16(B, B), b16(B, B), pltpu.SemaphoreType.DMA((4,))]
    outs = like(factors, cur, following) if far else like(factors, following)
    kernel = functools.partial(update_kernel if far else near_kernel, step, far)
    return call(kernel, outs, scratch, {1: 0, 2: 1} if far else {1: 0}, factors, cur, upper, received, scal=scal) if far else call(
        kernel, outs, scratch, {1: 0}, factors, upper, received, scal=scal)


def near_kernel(step, far, scal, factors_in, upper_in, received, factors, following, *scratch):
    update_kernel(step, far, scal, factors_in, None, upper_in, received, factors, None, following, *scratch)


def put_in_place(scal, upper, parts):
    scratch = [f32(B, B), pltpu.SemaphoreType.DMA((8,))]
    return call(place_kernel, like(upper), scratch, {1: 0}, upper, *parts, scal=scal)[0]


def put_swapped(scal, factors, upper, picks):
    scratch = [f32(B, B), f32(SHARE, B), pltpu.VMEM((SHARE, 128), jnp.int32), pltpu.SemaphoreType.DMA((2,))]
    return call(swap_kernel, like(factors), scratch, {1: 0}, factors, upper, picks, scal=scal)[0]


def gather(share):
    swap = [(r, r ^ 1) for r in range(ROWS)]
    turned = [lax.ppermute(share, "row", [(r, (r + 2 * turn) % ROWS) for r in range(ROWS)]) for turn in (1, 2, 3)]
    beside = lax.ppermute(share, "row", swap)
    *turned, beside = lax.optimization_barrier((*turned, beside))
    return [share, *turned, beside] + [lax.ppermute(part, "row", swap) for part in turned]


def send(cur, step, table):
    first = step % TILE - TILE
    pairs = []
    for at in range(first, PANELS + TILE, TILE):
        for distance, (_, sender) in table.items():
            if at + sender in range(PANELS) and at + distance in range(PANELS):
                pairs += [((at + sender) * ROWS + r, (at + distance) * ROWS + r) for r in range(ROWS)]
    return lax.ppermute(cur, ("col", "row"), pairs)


def members(step, tables):
    takers = sorted({
        step + d for table in tables for d, (lag, _) in table.items() if step - lag >= 0 and step + d < PANELS
    })
    inside = set(takers)
    grown = True
    while grown:
        grown = False
        for table in tables:
            for distance, (_, sender) in table.items():
                pair = {step + sender, step + distance}
                if pair <= set(range(PANELS)) and pair & inside and not pair <= inside:
                    inside |= pair
                    grown = True
    return takers, sorted(inside)


def shifted(amount, group):
    return [
        (c * ROWS + r, (c + amount) * ROWS + r)
        for c in range(PANELS - amount) if c // amount % 2 == group for r in range(ROWS)
    ]


def among(panel, panels):
    hit = panel == panels[0]
    for other in panels[1:]:
        hit = hit | (panel == other)
    return hit


def local(matrix, pivots, seeds):
    panel = lax.axis_index("col").astype(jnp.int32)
    place = lax.axis_index("row").astype(jnp.int32)
    factors = matrix.reshape(-1, B)
    own_pivots = lax.dynamic_index_in_dim(pivots, panel, 0, keepdims=False)
    onehot = (own_pivots[:, None] == jnp.arange(B, dtype=jnp.int32)[None, :]).astype(jnp.float32)
    start = jnp.dot(seeds[0], onehot, precision=lax.Precision.HIGHEST, preferred_element_type=jnp.float32)
    half = jax.ShapeDtypeStruct((B, B), jnp.bfloat16)
    y_high, y_low = call(halves_kernel, [half, half], [f32(B, B), b16(B, B), b16(B, B), pltpu.SemaphoreType.DMA((2,))], {}, start)
    picks = jnp.broadcast_to(
        lax.dynamic_slice_in_dim(pivots, place * SHARE, SHARE, 1)[:, :, None], (PANELS, SHARE, 128)
    )
    first = jnp.maximum(panel - HB, 0)
    following = lax.dynamic_slice_in_dim(factors, first * SHARE, SHARE, 0)
    cur = jnp.zeros((TALL, B), jnp.float32)
    front = jnp.zeros((SHARE, B), jnp.float32)
    where = jnp.stack([panel, place])

    def when(panels, run, *state):
        if not panels:
            return state
        return lax.cond(among(panel, panels), lambda *state: tuple(run(*state)), lambda *state: state, *state)

    def collect(upper, following):
        return put_in_place(where, upper, gather(following))

    def store_swapped(source, factors, upper):
        return put_swapped(jnp.stack([panel, place, source]), factors, upper, picks)

    upper = jnp.zeros((B, B), jnp.float32)
    fresh = jnp.zeros((B, B), jnp.float32)

    def prepare(factors, upper):
        upper = collect(upper, following)
        return store_swapped(jnp.int32(0), factors, upper), upper

    factors, upper = when([0, 1], prepare, factors, upper)

    def begin(factors, cur, front):
        return multiply(0, factors, cur, front, upper, cur, *inverse(upper, y_high, y_low))

    factors, cur, front = when([0], begin, factors, cur, front)

    for step in range(PANELS - 1):
        coming = step + 1

        def lead(following):
            arrived = lax.ppermute(front, ("col", "row"), shifted(1, step % 2))
            return (advance(step, factors, following, upper, arrived),)

        (following,) = when([step, coming], lead, following)
        near, _ = members(step, [NEAR])
        far, _ = members(step, [FAR])
        _, inside = members(step, [NEAR, FAR])

        def exchange(factors, cur, front, upper, fresh, following):
            p = send(cur, step, NEAR)
            q = send(cur, step, FAR) if far else None
            source = jnp.maximum(step - lag_of(step, FAR | NEAR, panel), 0)
            takers = sorted(set(near) | set(far))

            (fresh,) = when(takers, lambda fresh: (collect(fresh, following),), fresh)
            high, low = inverse(fresh, y_high, y_low)
            others = [c for c in takers if c != coming]
            mine = panel == step
            stored = jnp.where(among(panel, others), source, -1) if others else jnp.int32(-1)
            if step:
                stored = jnp.where(mine, step, stored)
                factors = store_swapped(jnp.where(mine, step - 1, -1), factors, upper)
            factors = store_swapped(stored, factors, fresh)

            def near_update(factors, following):
                return update(step, False, where, factors, cur, following, fresh, p)

            factors, following = when([c for c in near if c != coming], near_update, factors, following)

            def again(factors, fresh):
                fresh = collect(fresh, following)
                return store_swapped(source + 1, factors, fresh), fresh

            factors, fresh = when(sorted(set(near) & set(far)), again, factors, fresh)

            def far_next(factors, cur, upper, following):
                row = advance(step, factors, following, fresh, q)
                parts = gather(row)
                factors, cur, following = update(step, True, where, factors, cur, following, fresh, q)
                return factors, cur, put_in_place(where, upper, parts), following

            def far_update(factors, cur, following):
                return update(step, True, where, factors, cur, following, fresh, q)

            if far:
                factors, cur, upper, following = when([step + 2], far_next, factors, cur, upper, following)
                factors, cur, following = when([c for c in far if c != step + 2], far_update, factors, cur, following)

            def own(factors, cur, front):
                return multiply(coming, factors, cur, front, upper, p, high, low)

            factors, cur, front = when([coming], own, factors, cur, front)
            return factors, cur, front, upper, fresh, following

        factors, cur, front, upper, fresh, following = when(
            inside, exchange, factors, cur, front, upper, fresh, following
        )
    last = PANELS - 1
    factors = store_swapped(jnp.where(panel == last, last, -1), factors, fresh)
    factors = store_swapped(jnp.where(panel == last, last - 1, -1), factors, upper)
    at = (panel + 1) * SHARE
    own = lax.dynamic_slice_in_dim(factors, at, TALL, 0)
    own = lax.dot_general(
        own, onehot, (((1,), (1,)), ((), ())), precision=lax.Precision.HIGHEST, preferred_element_type=jnp.float32
    )
    factors = lax.dynamic_update_slice_in_dim(factors, own, at, 0)
    return factors.reshape(matrix.shape)


def solution(mesh):
    return jax.shard_map(
        local,
        mesh=mesh,
        in_specs=(P(None, "row", "col"), P(), P("col", None, None)),
        out_specs=P(None, "row", "col"),
        check_vma=False,
    )
```

```python
import functools

import jax
import jax.numpy as jnp
from jax import lax
from jax.experimental import pallas as pl
from jax.experimental.pallas import tpu as pltpu
from jax.sharding import PartitionSpec as P

HB = 8
PANELS = 16
B = 512
ROWS = 8
SHARE = B // ROWS
TALL = HB * SHARE
TILE = 9

NEAR = {1: (0, 0), 2: (1, -1), 3: (2, -2), 4: (2, 2)}
FAR = {2: (0, 0), 3: (1, -1), 5: (2, -2), 6: (2, 2)}


def split(value):
    high = value.astype(jnp.bfloat16)
    low = (value - high.astype(jnp.float32)).astype(jnp.bfloat16)
    return high, low


def dot(left, right):
    return jnp.dot(left, right, preferred_element_type=jnp.float32)


def dot3(left, right):
    return dot(left[0], right[0]) + (dot(left[0], right[1]) + dot(left[1], right[0]))


def exact_rows(onehot, value):
    high = value.astype(jnp.bfloat16)
    rest = value - high.astype(jnp.float32)
    mid = rest.astype(jnp.bfloat16)
    low = (rest - mid.astype(jnp.float32)).astype(jnp.bfloat16)
    return dot(onehot, high) + (dot(onehot, mid) + dot(onehot, low))


def split_into(value, high, low):
    def rows(index, _):
        block = pl.ds(pl.multiple_of(index * SHARE, SHARE), SHARE)
        high[block], low[block] = split(value[block])
        return 0

    lax.fori_loop(0, B // SHARE, rows, 0)


def halves_kernel(value_ref, high_ref, low_ref, value, high, low, sems):
    load = pltpu.make_async_copy(value_ref, value, sems.at[0])
    load.start()
    load.wait()
    split_into(value, high, low)
    store = [pltpu.make_async_copy(high, high_ref, sems.at[0]), pltpu.make_async_copy(low, low_ref, sems.at[1])]
    for copy in store:
        copy.start()
    for copy in store:
        copy.wait()


def inverse_kernel(pivot_ref, y_high_ref, y_low_ref, high_ref, low_ref,
                   pivot, y_high, y_low, high, low, other_high, other_low, result, sems):
    load = [
        pltpu.make_async_copy(pivot_ref, pivot, sems.at[0]),
        pltpu.make_async_copy(y_high_ref, y_high, sems.at[1]),
        pltpu.make_async_copy(y_low_ref, y_low, sems.at[2]),
    ]
    for copy in load:
        copy.start()
    for copy in load:
        copy.wait()
    chunk = 128

    def errors(index, _):
        first = pl.multiple_of(index * chunk, chunk)
        block = pl.ds(first, chunk)
        product = dot3(split(pivot[block]), (y_high[...], y_low[...]))
        row_ids = lax.broadcasted_iota(jnp.int32, (chunk, B), 0) + first
        col_ids = lax.broadcasted_iota(jnp.int32, (chunk, B), 1)
        high[block], low[block] = split(jnp.where(row_ids == col_ids, 1.0, 0.0) - product)
        return 0

    def squares(index, _):
        block = pl.ds(pl.multiple_of(index * chunk, chunk), chunk)
        other_high[block], other_low[block] = split(dot3((high[block], low[block]), (high[...], low[...])))
        base = y_high[block].astype(jnp.float32) + y_low[block].astype(jnp.float32)
        result[block] = base + dot3((y_high[block], y_low[block]), (high[...], low[...]))
        return 0

    def inverses(index, _):
        block = pl.ds(pl.multiple_of(index * chunk, chunk), chunk)
        base = result[block]
        high[block], low[block] = split(base + dot3(split(base), (other_high[...], other_low[...])))
        return 0

    lax.fori_loop(0, B // chunk, errors, 0)
    lax.fori_loop(0, B // chunk, squares, 0)
    lax.fori_loop(0, B // chunk, inverses, 0)
    store = [pltpu.make_async_copy(high, high_ref, sems.at[0]), pltpu.make_async_copy(low, low_ref, sems.at[1])]
    for copy in store:
        copy.start()
    for copy in store:
        copy.wait()


def multiply_kernel(owner, factors_in, cur_in, upper_in, received, high_ref, low_ref, factors, cur, front,
                    upper, multipliers, below, high, low, upper_high, upper_low, sems):
    rows = pl.ds((owner + 1) * SHARE, TALL)
    load = [
        pltpu.make_async_copy(factors_in.at[rows], below, sems.at[0]),
        pltpu.make_async_copy(high_ref, high, sems.at[1]),
        pltpu.make_async_copy(low_ref, low, sems.at[2]),
    ]
    if owner:
        load += [
            pltpu.make_async_copy(upper_in, upper, sems.at[3]),
            pltpu.make_async_copy(received, multipliers, sems.at[4]),
        ]
    for copy in load:
        copy.start()
    if owner:
        load[3].wait()
        split_into(upper, upper_high, upper_low)
    for copy in load[:3] + load[4:]:
        copy.wait()
    if owner:
        chunk = (TALL - SHARE) // 2

        def subtract(index, _):
            first = pl.multiple_of(index * chunk, 32)
            block = pl.ds(first, chunk)
            shifted = pl.ds(pl.multiple_of(first + SHARE, 32), chunk)
            below[block] = below[block] - dot3(split(multipliers[shifted]), (upper_high[...], upper_low[...]))
            return 0

        lax.fori_loop(0, 2, subtract, 0)
    part = 128

    def multiply(index, _):
        block = pl.ds(pl.multiple_of(index * part, part), part)
        below[block] = dot3(split(below[block]), (high[...], low[...]))
        return 0

    lax.fori_loop(0, TALL // part, multiply, 0)
    store = [
        pltpu.make_async_copy(below.at[pl.ds(0, SHARE)], front, sems.at[0]),
        pltpu.make_async_copy(below, cur, sems.at[1]),
        pltpu.make_async_copy(below, factors.at[rows], sems.at[2]),
    ]
    for copy in store:
        copy.start()
    for copy in store:
        copy.wait()


def front_kernel(step, factors_in, upper_in, received, following, upper, multipliers, target, high, low, sems):
    rows = pl.ds((step + 1) * SHARE, SHARE)
    load = [
        pltpu.make_async_copy(upper_in, upper, sems.at[0]),
        pltpu.make_async_copy(received.at[pl.ds(0, SHARE)], multipliers, sems.at[1]),
        pltpu.make_async_copy(factors_in.at[rows], target, sems.at[2]),
    ]
    for copy in load:
        copy.start()
    for copy in load:
        copy.wait()
    left = split(multipliers[...])
    split_into(upper, high, low)
    target[...] = target[...] - dot3(left, (high[...], low[...]))
    store = pltpu.make_async_copy(target, following, sems.at[0])
    store.start()
    store.wait()


def lag_of(step, table, panel):
    lag = jnp.int32(0)
    for distance, (amount, _) in table.items():
        if amount:
            lag = jnp.where(panel == step + distance, amount, lag)
    return lag


def update_kernel(step, far, scal, factors_in, cur_in, upper_in, received, factors, cur, following,
                  upper, multipliers, target, high, low, sems):
    panel = scal[0]
    source = step - lag_of(step, FAR if far else NEAR, panel)
    rows = pl.ds(pl.multiple_of((source + 1) * SHARE, SHARE), TALL)
    load = [
        pltpu.make_async_copy(upper_in, upper, sems.at[0]),
        pltpu.make_async_copy(received, multipliers, sems.at[1]),
        pltpu.make_async_copy(factors_in.at[rows], target, sems.at[2]),
    ]
    for copy in load:
        copy.start()
    load[0].wait()
    split_into(upper, high, low)
    load[1].wait()
    if far:
        keep = pltpu.make_async_copy(multipliers, cur, sems.at[3])
        keep.start()
    load[2].wait()
    chunk = 128

    def subtract(index, _):
        block = pl.ds(pl.multiple_of(index * chunk, chunk), chunk)
        target[block] = target[block] - dot3(split(multipliers[block]), (high[...], low[...]))
        return 0

    lax.fori_loop(0, TALL // chunk, subtract, 0)
    store = [
        pltpu.make_async_copy(target.at[pl.ds(0, SHARE)], following, sems.at[0]),
        pltpu.make_async_copy(target, factors.at[rows], sems.at[1]),
    ]
    for copy in store:
        copy.start()
    for copy in store:
        copy.wait()
    if far:
        keep.wait()


def place_kernel(scal, upper_in, *rest):
    parts, (upper_out, upper, sems) = rest[:8], rest[8:]
    del upper_in
    place = scal[1]
    z = place // 2
    core = place % 2
    load = []
    for index, part in enumerate(parts):
        other = core if index < 4 else 1 - core
        offset = (2 * ((z + 4 - index % 4) % 4) + other) * SHARE
        at = pl.ds(pl.multiple_of(offset, SHARE), SHARE)
        load.append(pltpu.make_async_copy(part, upper.at[at], sems.at[index]))
    for copy in load:
        copy.start()
    for copy in load:
        copy.wait()
    keep = pltpu.make_async_copy(upper, upper_out, sems.at[0])
    keep.start()
    keep.wait()


def swap_kernel(scal, factors_in, upper_in, pivot_ref, factors, upper, swapped, picks, sems):
    del factors_in
    source = scal[2]

    @pl.when(source >= 0)
    def _():
        load = [
            pltpu.make_async_copy(upper_in, upper, sems.at[0]),
            pltpu.make_async_copy(pivot_ref.at[source], picks, sems.at[1]),
        ]
        for copy in load:
            copy.start()
        for copy in load:
            copy.wait()
        lanes = lax.broadcasted_iota(jnp.int32, (SHARE, 128), 1)
        swapped[...] = jnp.zeros_like(swapped)

        def pick_rows(group, _):
            onehot = jnp.where(picks[...] == lanes + 128 * group, 1.0, 0.0).astype(jnp.bfloat16)
            block = pl.ds(pl.multiple_of(group * 128, 128), 128)
            swapped[...] = swapped[...] + exact_rows(onehot, upper[block])
            return 0

        lax.fori_loop(0, B // 128, pick_rows, 0)
        at = pl.ds(pl.multiple_of(source * SHARE, SHARE), SHARE)
        store = pltpu.make_async_copy(swapped, factors.at[at], sems.at[0])
        store.start()
        store.wait()


ANY = pl.BlockSpec(memory_space=pl.ANY)
SMEM = pl.BlockSpec(memory_space=pltpu.SMEM)
HBM = pl.BlockSpec(memory_space=pltpu.HBM)


def f32(*shape):
    return pltpu.VMEM(shape, jnp.float32)


def b16(*shape):
    return pltpu.VMEM(shape, jnp.bfloat16)


def like(*arrays):
    return [jax.ShapeDtypeStruct(a.shape, a.dtype) for a in arrays]


def space(array):
    return HBM if array.shape[0] > TALL else ANY


def call(kernel, out_shape, scratch, aliases, *operands, scal=None):
    first = [] if scal is None else [scal]
    return pl.pallas_call(
        kernel,
        out_shape=out_shape,
        in_specs=[SMEM] * len(first) + [space(a) for a in operands],
        out_specs=[space(a) for a in out_shape],
        scratch_shapes=scratch,
        input_output_aliases=aliases,
        compiler_params=pltpu.CompilerParams(vmem_limit_bytes=48 << 20),
    )(*first, *operands)


def inverse(pivot, y_high, y_low):
    scratch = [f32(B, B)] + [b16(B, B)] * 6 + [f32(B, B), pltpu.SemaphoreType.DMA((3,))]
    return call(inverse_kernel, like(y_high, y_low), scratch, {}, pivot, y_high, y_low)


def multiply(owner, factors, cur, front, upper, received, high, low):
    scratch = [f32(B, B), f32(TALL, B), f32(TALL, B)] + [b16(B, B)] * 4 + [pltpu.SemaphoreType.DMA((5,))]
    return call(functools.partial(multiply_kernel, owner), like(factors, cur, front), scratch, {0: 0, 1: 1},
                factors, cur, upper, received, high, low)


def advance(step, factors, following, upper, received):
    scratch = [f32(B, B), f32(SHARE, B), f32(SHARE, B), b16(B, B), b16(B, B), pltpu.SemaphoreType.DMA((3,))]
    return call(functools.partial(front_kernel, step), like(following), scratch, {}, factors, upper, received)[0]


def update(step, far, scal, factors, cur, following, upper, received):
    scratch = [f32(B, B), f32(TALL, B), f32(TALL, B), b16(B, B), b16(B, B), pltpu.SemaphoreType.DMA((4,))]
    outs = like(factors, cur, following) if far else like(factors, following)
    kernel = functools.partial(update_kernel if far else near_kernel, step, far)
    return call(kernel, outs, scratch, {1: 0, 2: 1} if far else {1: 0}, factors, cur, upper, received, scal=scal) if far else call(
        kernel, outs, scratch, {1: 0}, factors, upper, received, scal=scal)


def near_kernel(step, far, scal, factors_in, upper_in, received, factors, following, *scratch):
    update_kernel(step, far, scal, factors_in, None, upper_in, received, factors, None, following, *scratch)


def put_in_place(scal, upper, parts):
    scratch = [f32(B, B), pltpu.SemaphoreType.DMA((8,))]
    return call(place_kernel, like(upper), scratch, {1: 0}, upper, *parts, scal=scal)[0]


def put_swapped(scal, factors, upper, picks):
    scratch = [f32(B, B), f32(SHARE, B), pltpu.VMEM((SHARE, 128), jnp.int32), pltpu.SemaphoreType.DMA((2,))]
    return call(swap_kernel, like(factors), scratch, {1: 0}, factors, upper, picks, scal=scal)[0]


def gather(share):
    swap = [(r, r ^ 1) for r in range(ROWS)]
    turned = [lax.ppermute(share, "row", [(r, (r + 2 * turn) % ROWS) for r in range(ROWS)]) for turn in (1, 2, 3)]
    beside = lax.ppermute(share, "row", swap)
    *turned, beside = lax.optimization_barrier((*turned, beside))
    return [share, *turned, beside] + [lax.ppermute(part, "row", swap) for part in turned]


def send(cur, step, table):
    first = step % TILE - TILE
    pairs = []
    for at in range(first, PANELS + TILE, TILE):
        for distance, (_, sender) in table.items():
            if at + sender in range(PANELS) and at + distance in range(PANELS):
                pairs += [((at + sender) * ROWS + r, (at + distance) * ROWS + r) for r in range(ROWS)]
    return lax.ppermute(cur, ("col", "row"), pairs)


def members(step, tables):
    takers = sorted({
        step + d for table in tables for d, (lag, _) in table.items() if step - lag >= 0 and step + d < PANELS
    })
    inside = set(takers)
    grown = True
    while grown:
        grown = False
        for table in tables:
            for distance, (_, sender) in table.items():
                pair = {step + sender, step + distance}
                if pair <= set(range(PANELS)) and pair & inside and not pair <= inside:
                    inside |= pair
                    grown = True
    return takers, sorted(inside)


def shifted(amount, group):
    return [
        (c * ROWS + r, (c + amount) * ROWS + r)
        for c in range(PANELS - amount) if c // amount % 2 == group for r in range(ROWS)
    ]


def among(panel, panels):
    hit = panel == panels[0]
    for other in panels[1:]:
        hit = hit | (panel == other)
    return hit


def local(matrix, pivots, seeds):
    panel = lax.axis_index("col").astype(jnp.int32)
    place = lax.axis_index("row").astype(jnp.int32)
    factors = matrix.reshape(-1, B)
    own_pivots = lax.dynamic_index_in_dim(pivots, panel, 0, keepdims=False)
    onehot = (own_pivots[:, None] == jnp.arange(B, dtype=jnp.int32)[None, :]).astype(jnp.float32)
    start = jnp.dot(seeds[0], onehot, precision=lax.Precision.HIGHEST, preferred_element_type=jnp.float32)
    half = jax.ShapeDtypeStruct((B, B), jnp.bfloat16)
    y_high, y_low = call(halves_kernel, [half, half], [f32(B, B), b16(B, B), b16(B, B), pltpu.SemaphoreType.DMA((2,))], {}, start)
    picks = jnp.broadcast_to(
        lax.dynamic_slice_in_dim(pivots, place * SHARE, SHARE, 1)[:, :, None], (PANELS, SHARE, 128)
    )
    first = jnp.maximum(panel - HB, 0)
    following = lax.dynamic_slice_in_dim(factors, first * SHARE, SHARE, 0)
    cur = jnp.zeros((TALL, B), jnp.float32)
    front = jnp.zeros((SHARE, B), jnp.float32)
    where = jnp.stack([panel, place])

    def when(panels, run, *state):
        if not panels:
            return state
        return lax.cond(among(panel, panels), lambda *state: tuple(run(*state)), lambda *state: state, *state)

    def collect(upper, following):
        return put_in_place(where, upper, gather(following))

    def store_swapped(source, factors, upper):
        return put_swapped(jnp.stack([panel, place, source]), factors, upper, picks)

    upper = jnp.zeros((B, B), jnp.float32)
    fresh = jnp.zeros((B, B), jnp.float32)

    def prepare(factors, upper):
        upper = collect(upper, following)
        return store_swapped(jnp.int32(0), factors, upper), upper

    factors, upper = when([0, 1], prepare, factors, upper)

    def begin(factors, cur, front):
        return multiply(0, factors, cur, front, upper, cur, *inverse(upper, y_high, y_low))

    factors, cur, front = when([0], begin, factors, cur, front)

    for step in range(PANELS - 1):
        coming = step + 1

        def lead(following):
            arrived = lax.ppermute(front, ("col", "row"), shifted(1, step % 2))
            return (advance(step, factors, following, upper, arrived),)

        (following,) = when([step, coming], lead, following)
        near, _ = members(step, [NEAR])
        far, _ = members(step, [FAR])
        _, inside = members(step, [NEAR, FAR])

        def exchange(factors, cur, front, upper, fresh, following):
            p = send(cur, step, NEAR)
            q = send(cur, step, FAR) if far else None
            source = jnp.maximum(step - lag_of(step, FAR | NEAR, panel), 0)
            takers = sorted(set(near) | set(far))

            following, fresh = when(
                takers, lambda following, fresh: (following, collect(fresh, following)), following, fresh
            )
            high, low = inverse(fresh, y_high, y_low)
            factors, high, low = lax.optimization_barrier((factors, high, low))
            others = [c for c in takers if c != coming]
            mine = panel == step
            stored = jnp.where(among(panel, others), source, -1) if others else jnp.int32(-1)
            if step:
                stored = jnp.where(mine, step, stored)
                factors = store_swapped(jnp.where(mine, step - 1, -1), factors, upper)
            factors = store_swapped(stored, factors, fresh)

            def near_update(factors, following):
                return update(step, False, where, factors, cur, following, fresh, p)

            factors, following = when([c for c in near if c != coming], near_update, factors, following)

            def again(factors, fresh):
                fresh = collect(fresh, following)
                return store_swapped(source + 1, factors, fresh), fresh

            factors, fresh = when(sorted(set(near) & set(far)), again, factors, fresh)

            def far_update(factors, cur, following):
                return update(step, True, where, factors, cur, following, fresh, q)

            if far:
                factors, cur, following = when(far, far_update, factors, cur, following)
                following, upper = when(
                    [step + 2], lambda following, upper: (following, collect(upper, following)), following, upper
                )

            def own(factors, cur, front):
                return multiply(coming, factors, cur, front, upper, p, high, low)

            factors, cur, front = when([coming], own, factors, cur, front)
            return factors, cur, front, upper, fresh, following

        factors, cur, front, upper, fresh, following = when(
            inside, exchange, factors, cur, front, upper, fresh, following
        )
    last = PANELS - 1
    factors = store_swapped(jnp.where(panel == last, last, -1), factors, fresh)
    factors = store_swapped(jnp.where(panel == last, last - 1, -1), factors, upper)
    at = (panel + 1) * SHARE
    own = lax.dynamic_slice_in_dim(factors, at, TALL, 0)
    own = lax.dot_general(
        own, onehot, (((1,), (1,)), ((), ())), precision=lax.Precision.HIGHEST, preferred_element_type=jnp.float32
    )
    factors = lax.dynamic_update_slice_in_dim(factors, own, at, 0)
    return factors.reshape(matrix.shape)


def solution(mesh):
    return jax.shard_map(
        local,
        mesh=mesh,
        in_specs=(P(None, "row", "col"), P(), P("col", None, None)),
        out_specs=P(None, "row", "col"),
        check_vma=False,
    )
```
